256 devices in a mesh: gx: 8 (over z), gy: 4 (over y), gz: 8 (over x, core).
Axes of the slice: x: 4, y: 4, z: 8, core: 2. Of those that a mesh axis runs over, the one named last changes fastest.
Arguments:
- fine_state: float32 [512, 5, 32, 1024], P(('gx', 'gy', 'gz')), may hold values from -1.2 to 3.5, as said below
- coarse_state: float32 [2048, 5, 16, 256], P(('gx', 'gy', 'gz')), may hold values from -1.2 to 3.5, as said below
- neighbours: int32 [512, 6], P(('gx', 'gy', 'gz')), may hold values from -1 to 511, as said below
- coarse_sources: int32 [512, 6], P(('gx', 'gy', 'gz')), may hold values from -1 to 2047, as said below
- covering: int32 [2048], P(('gx', 'gy', 'gz')), may hold values from -1 to 511, as said below
Outputs:
- fine_next: float32 [512, 5, 32, 1024], P(('gx', 'gy', 'gz'))
- coarse_next: float32 [2048, 5, 16, 256], P(('gx', 'gy', 'gz'))
The draws below stay inside these ranges and needn't reach their ends.
Inputs may be any that keep to these rules, and one draw needn't show every extreme that they name: `fine_state`: each cell is the conserved state of density 0.5 to 2, velocity components -0.6 to 0.6 and pressure 0.4 to 1.6. `coarse_state`: each cell is the conserved state of density 0.5 to 2, velocity components -0.6 to 0.6 and pressure 0.4 to 1.6. For each box face exactly one of neighbours and coarse_sources is not -1; every box or block named lies on a device with the same gx index as the box; the faces of one device's boxes name at most 1 boxes or blocks held by any one device, and exactly 1 on some device. `coarse_sources`: see neighbours. `covering`: every fine box is named by exactly one block; a block and the box it names lie on devices with the same gy and gz index; the blocks of one device name at most 1 boxes of any one device, and exactly 1 of some device.
All inputs are finite; a program needn't handle non-finite values.
Results may differ from the reference program's by a relative error of at most 0.00005.
Values sent between devices are 32-bit elements; how exact they have to be, the bound alone decides.
No kernel may reach another device: no remote copies, remote signals or barrier semaphores. Data moves between devices by JAX's collectives and lax.ppermute only.
A program may use at most 64 MiB of HBM per device.

```python
import math
import jax
import jax.numpy as jnp
from jax import lax

EDGE = 32
HALF = 16
BOX_DEV = 2
CB_DEV = 8
BOXES = 512
CBLOCKS = 2048
N_GX = 8
N_GY = 4
N_GZ = 8
DEVICES = 256


adiabatic = 5.0 / 3.0


def conserved(key, item_count, row_count, width):
    subkeys = jax.random.split(key, 3)
    cell_shape = (item_count, row_count, width)
    density = jnp.exp(jax.random.uniform(subkeys[0], cell_shape, jnp.float32, math.log(0.5), math.log(2.0)))
    velocity = 0.25 * jax.random.truncated_normal(subkeys[1], -2.4, 2.4, (3,) + cell_shape, jnp.float32)
    pressure = jnp.exp(jax.random.uniform(subkeys[2], cell_shape, jnp.float32, math.log(0.4), math.log(1.6)))
    momentum = density[None] * velocity
    energy = pressure / (adiabatic - 1.0) + 0.5 * density * jnp.sum(velocity * velocity, axis=0)
    return jnp.stack([density, momentum[0], momentum[1], momentum[2], energy], axis=1)


def draw_fine_state(key, part):
    return conserved(jax.random.fold_in(key, 3), BOXES, EDGE, EDGE * EDGE)


def draw_coarse_state(key, part):
    return conserved(jax.random.fold_in(key, 5), CBLOCKS, HALF, HALF * HALF)


def face_sources(key):
    line_size = N_GY * N_GZ
    face_count = 6 * BOX_DEV
    per_peer = (face_count + line_size - 1) // line_size
    subkeys = jax.random.split(jax.random.fold_in(key, 11), 5)
    peer_keys = jax.random.split(subkeys[0], DEVICES)
    peer_order = jax.vmap(lambda subkey: jax.random.permutation(subkey, line_size))(peer_keys)
    face_keys = jax.random.split(subkeys[1], DEVICES)
    face_order = jax.vmap(lambda subkey: jax.random.permutation(subkey, face_count))(face_keys)
    sequence = jnp.broadcast_to(jnp.arange(face_count, dtype=jnp.int32) // per_peer, (DEVICES, face_count))
    peer_seq = jnp.take_along_axis(peer_order, sequence, axis=1)
    peer_face = jnp.take_along_axis(peer_seq, jnp.argsort(face_order, axis=1), axis=1)
    devices = jnp.arange(DEVICES, dtype=jnp.int32)
    source_dev = (devices // line_size)[:, None] * line_size + peer_face
    fine_face = jax.random.randint(subkeys[2], (DEVICES, face_count), 0, 2)
    fine_pick = jax.random.randint(subkeys[3], (DEVICES, face_count), 0, BOX_DEV)
    coarse_pick = jax.random.randint(subkeys[4], (DEVICES, face_count), 0, CB_DEV)
    fine_ids = jnp.where(fine_face == 1, source_dev * BOX_DEV + fine_pick, -1)
    coarse_ids = jnp.where(fine_face == 0, source_dev * CB_DEV + coarse_pick, -1)
    return (fine_ids.reshape(BOXES, 6).astype(jnp.int32), coarse_ids.reshape(BOXES, 6).astype(jnp.int32))


def draw_neighbours(key, part):
    return face_sources(key)[0]


def draw_coarse_sources(key, part):
    return face_sources(key)[1]


def draw_covering(key, part):
    line_size = N_GY * N_GZ
    per_pair = (BOX_DEV + N_GX - 1) // N_GX
    subkeys = jax.random.split(jax.random.fold_in(key, 23), 4)
    weight = 1 + jax.random.randint(subkeys[0], (line_size, 1, N_GX), 0, 4) ** 2
    scores = jax.random.randint(subkeys[1], (line_size, N_GX, N_GX), 0, 1024) * weight
    scores = scores * N_GX + jnp.arange(N_GX, dtype=jnp.int32)
    target_order = jnp.argsort(-scores, axis=2)
    pick_index = jnp.arange(BOX_DEV, dtype=jnp.int32) // per_pair
    target = target_order[:, :, pick_index]
    slot_keys = jax.random.split(subkeys[2], line_size * N_GX)
    slot_order = jax.vmap(lambda subkey: jax.random.permutation(subkey, BOX_DEV))(slot_keys).reshape(line_size, N_GX * BOX_DEV)
    flat_target = target.reshape(line_size, N_GX * BOX_DEV)
    hits = (flat_target[:, :, None] == jnp.arange(N_GX, dtype=jnp.int32)[None, None, :]).astype(jnp.int32)
    arrival = jnp.sum((jnp.cumsum(hits, axis=1) - hits) * hits, axis=2)
    block_keys = jax.random.split(subkeys[3], line_size * N_GX)
    block_order = jax.vmap(lambda subkey: jax.random.permutation(subkey, CB_DEV))(block_keys).reshape(line_size, N_GX, CB_DEV)
    lines = jnp.arange(line_size, dtype=jnp.int32)[:, None]
    block_slot = block_order[lines, flat_target, arrival]
    sender = jnp.broadcast_to(jnp.arange(N_GX, dtype=jnp.int32)[None, :, None], (line_size, N_GX, BOX_DEV)).reshape(line_size, N_GX * BOX_DEV)
    fine_ids = (sender * line_size + lines) * BOX_DEV + slot_order
    coarse_rows = (flat_target * line_size + lines) * CB_DEV + block_slot
    covering = jnp.full((CBLOCKS,), -1, jnp.int32)
    return covering.at[coarse_rows.reshape(-1)].set(fine_ids.reshape(-1).astype(jnp.int32))


def setup_inputs(seed: int = 0) -> dict:
    splits = jax.random.split(jax.random.key(seed), 6)
    return {
        "fine_state": draw_fine_state(jax.random.fold_in(splits[5], 71), 0),
        "coarse_state": draw_coarse_state(jax.random.fold_in(splits[5], 71), 0),
        "neighbours": draw_neighbours(jax.random.fold_in(splits[5], 71), 0),
        "coarse_sources": draw_coarse_sources(jax.random.fold_in(splits[5], 71), 0),
        "covering": draw_covering(jax.random.fold_in(splits[5], 71), 0),
    }


adiabatic = 5.0 / 3.0
courant = 0.12

def edge_flux(left_state, right_state, normal):
    fluxes = []
    speeds = []
    for current in (left_state, right_state):
        density = current[0]
        normal_speed = current[normal] / density
        kinetic = 0.5 * (current[1] * current[1] + current[2] * current[2] + current[3] * current[3]) / density
        pressure = (adiabatic - 1.0) * (current[4] - kinetic)
        sound_speed = jnp.sqrt(adiabatic * pressure / density)
        entries = [current[normal], current[1] * normal_speed, current[2] * normal_speed, current[3] * normal_speed, (current[4] + pressure) * normal_speed]
        entries[normal] = entries[normal] + pressure
        fluxes.append(jnp.stack(entries))
        speeds.append(jnp.abs(normal_speed) + sound_speed)
    fastest = jnp.maximum(speeds[0], speeds[1])
    return 0.5 * (fluxes[0] + fluxes[1]) - 0.5 * fastest * (right_state - left_state)

def face_layers(cubes):
    return [cubes[:, :, 0], cubes[:, :, -1], cubes[:, :, :, 0], cubes[:, :, :, -1], cubes[:, :, :, :, 0], cubes[:, :, :, :, -1]]

def advance(box_cells, ghosts):
    padded = jnp.pad(box_cells, ((0, 0), (1, 1), (1, 1), (1, 1)))
    padded = padded.at[:, 0, 1:-1, 1:-1].set(ghosts[0])
    padded = padded.at[:, -1, 1:-1, 1:-1].set(ghosts[1])
    padded = padded.at[:, 1:-1, 0, 1:-1].set(ghosts[2])
    padded = padded.at[:, 1:-1, -1, 1:-1].set(ghosts[3])
    padded = padded.at[:, 1:-1, 1:-1, 0].set(ghosts[4])
    padded = padded.at[:, 1:-1, 1:-1, -1].set(ghosts[5])
    flux_x = edge_flux(padded[:, :-1, 1:-1, 1:-1], padded[:, 1:, 1:-1, 1:-1], 1)
    step_x = flux_x[:, 1:] - flux_x[:, :-1]
    flux_y = edge_flux(padded[:, 1:-1, :-1, 1:-1], padded[:, 1:-1, 1:, 1:-1], 2)
    step_y = flux_y[:, :, 1:] - flux_y[:, :, :-1]
    flux_z = edge_flux(padded[:, 1:-1, 1:-1, :-1], padded[:, 1:-1, 1:-1, 1:], 3)
    step_z = flux_z[:, :, :, 1:] - flux_z[:, :, :, :-1]
    return box_cells - courant * (step_x + step_y + step_z)

def reference(fine_state, coarse_state, neighbours, coarse_sources, covering):
    fine_cubes = fine_state.reshape(BOXES, 5, EDGE, EDGE, EDGE)
    coarse_cubes = coarse_state.reshape(CBLOCKS, 5, HALF, HALF, HALF)
    fine_faces = face_layers(fine_cubes)
    coarse_faces = [jnp.repeat(jnp.repeat(layer, 2, axis=2), 2, axis=3) for layer in face_layers(coarse_cubes)]
    ghost_list = []
    for face_side in range(6):
        opposite = face_side ^ 1
        from_fine = jnp.take(fine_faces[opposite], jnp.maximum(neighbours[:, face_side], 0), axis=0)
        from_coarse = jnp.take(coarse_faces[opposite], jnp.maximum(coarse_sources[:, face_side], 0), axis=0)
        ghost_list.append(jnp.where(neighbours[:, face_side][:, None, None, None] >= 0, from_fine, from_coarse))
    updated = lax.map(lambda packed: advance(packed[0], packed[1:]), (fine_cubes,) + tuple(ghost_list))
    averaged = updated.reshape(BOXES, 5, HALF, 2, HALF, 2, HALF, 2).mean(axis=(3, 5, 7))
    picked = jnp.take(averaged, jnp.maximum(covering, 0), axis=0)
    coarse_next = jnp.where(covering[:, None, None, None, None] >= 0, picked, coarse_cubes)
    return (updated.reshape(BOXES, 5, EDGE, EDGE * EDGE), coarse_next.reshape(CBLOCKS, 5, HALF, HALF * HALF))
```

```python
import functools

import jax
import jax.numpy as jnp
from jax import lax
from jax.experimental import pallas as pl
from jax.experimental.pallas import tpu as pltpu
from jax.sharding import PartitionSpec as P

adiabatic = 5.0 / 3.0
courant = 0.12
AXES = ("gx", "gy", "gz")
PLANE = ("gy", "gz")

EDGE = 32
HALF = 16
FLAT = EDGE * EDGE
SMALL = HALF * HALF
LANES = 128
COMPS = 5
SLOT_ROWS = COMPS * FLAT // LANES


def iota(shape, dim):
    return lax.broadcasted_iota(jnp.int32, shape, dim)


def roll(x, shift, axis):
    size = x.shape[axis]
    shift = shift % size
    return x if shift == 0 else pltpu.roll(x, shift, axis)


def face_source(fine_ref, coarse_ref, box, side, boxes, blocks, line_size):
    fine_id = fine_ref[box, side]
    coarse_id = coarse_ref[box, side]
    is_fine = fine_id >= 0
    device = jnp.where(is_fine, lax.div(fine_id, boxes), lax.div(coarse_id, blocks))
    row = jnp.where(
        is_fine,
        lax.rem(fine_id, boxes) * 6 + (side ^ 1),
        boxes * 6 + lax.rem(coarse_id, blocks) * 6 + (side ^ 1),
    )
    return lax.rem(device, line_size), row


def request_kernel(boxes, blocks, line_size, fine_ref, coarse_ref, out_ref):
    peers = iota(out_ref.shape, 0)
    table = jnp.zeros(out_ref.shape, jnp.int32)
    for box in range(boxes):
        for side in range(6):
            peer, row = face_source(fine_ref, coarse_ref, box, side, boxes, blocks, line_size)
            table = jnp.where(peers == peer, row + 1, table)
    out_ref[...] = table


def lane_gather(x, index):
    return jnp.take_along_axis(x, index, axis=1)


def row_gather(x, index):
    return jnp.take_along_axis(x, index, axis=0)


def table_kernel(boxes, blocks, fine_ref, coarse_ref, out_ref):
    row = iota((8, LANES), 0)
    lane = iota((8, LANES), 1)
    quad = lane // 32
    inner = lane % 32

    def fine_box(box, _):
        base = box * 6
        for comp in range(COMPS):
            dst = slice(8 * comp, 8 * comp + 8)
            for side, first in ((0, 0), (1, EDGE - 1)):
                for r in range(8):
                    out_ref[base + side, 8 * comp + r : 8 * comp + r + 1, :] = fine_ref[
                        box, comp, first : first + 1, LANES * r : LANES * r + LANES
                    ]
            y_low = jnp.zeros((8, LANES), jnp.float32)
            y_high = y_low
            z_low = y_low
            z_high = y_low
            for q in range(4):
                for v in range(8):
                    cells = fine_ref[box, comp, 8 * q : 8 * q + 8, LANES * v : LANES * v + LANES]
                    if v == 0:
                        y_low = jnp.where(quad == q, roll(cells, 32 * q, 1), y_low)
                    if v == 7:
                        y_high = jnp.where(quad == q, roll(cells, 32 * q - 96, 1), y_high)
                    spot = inner == 8 * q + v
                    z_low = jnp.where(spot, roll(cells, 8 * q + v, 1), z_low)
                    z_high = jnp.where(spot, roll(cells, 8 * q + v - 31, 1), z_high)
            out_ref[base + 2, dst, :] = y_low
            out_ref[base + 3, dst, :] = y_high
            out_ref[base + 4, dst, :] = z_low
            out_ref[base + 5, dst, :] = z_high
        return 0

    lax.fori_loop(0, boxes, fine_box, 0)

    pick_x = 32 * (row % 4) + 16 * (quad // 2) + inner // 2
    pick_y = inner // 2
    pick_z = 32 * (inner % 4) + 16 * (quad // 2)
    rows_y = 4 * (quad % 2) + row // 2
    rows_z = 4 * ((inner // 8) % 2) + row // 2

    def coarse_block(block, _):
        base = boxes * 6 + block * 6
        for comp in range(COMPS):
            dst = slice(8 * comp, 8 * comp + 8)
            cells = [
                [
                    coarse_ref[block, comp, 8 * g : 8 * g + 8, LANES * h : LANES * h + LANES]
                    for h in range(2)
                ]
                for g in range(2)
            ]
            for side, first in ((0, 0), (1, HALF - 1)):
                parts = [
                    jnp.broadcast_to(cells[first // 8][h][first % 8 : first % 8 + 1], (8, LANES))
                    for h in range(2)
                ]
                out_ref[base + side, dst, :] = jnp.where(
                    row < 4, lane_gather(parts[0], pick_x), lane_gather(parts[1], pick_x)
                )
            for side, half, start in ((2, 0, 0), (3, 1, LANES - HALF)):
                parts = [
                    row_gather(lane_gather(cells[g][half], pick_y + start), rows_y)
                    for g in range(2)
                ]
                out_ref[base + side, dst, :] = jnp.where(quad < 2, parts[0], parts[1])
            for side, last in ((4, 0), (5, HALF - 1)):
                parts = [
                    row_gather(
                        jnp.where(
                            inner % 8 < 4,
                            lane_gather(cells[g][0], pick_z + last),
                            lane_gather(cells[g][1], pick_z + last),
                        ),
                        rows_z,
                    )
                    for g in range(2)
                ]
                out_ref[base + side, dst, :] = jnp.where(inner < 16, parts[0], parts[1])
        return 0

    lax.fori_loop(0, blocks, coarse_block, 0)


def primitives(cells):
    inverse = 1.0 / cells[0]
    kinetic = (
        0.5 * (cells[1] * cells[1] + cells[2] * cells[2] + cells[3] * cells[3]) * inverse
    )
    pressure = (adiabatic - 1.0) * (cells[4] - kinetic)
    sound = jnp.sqrt(adiabatic * pressure * inverse)
    return inverse, pressure, sound


def physical_flux(cells, normal, speed, pressure):
    entries = [
        cells[normal],
        cells[1] * speed,
        cells[2] * speed,
        cells[3] * speed,
        (cells[4] + pressure) * speed,
    ]
    entries[normal] = entries[normal] + pressure
    return entries


def scaled_flux(low, high, normal, low_state, high_state):
    low_speed, low_pressure, low_fast = low_state
    high_speed, high_pressure, high_fast = high_state
    fastest = jnp.maximum(low_fast, high_fast)
    low_flux = physical_flux(low, normal, low_speed, low_pressure)
    high_flux = physical_flux(high, normal, high_speed, high_pressure)
    return [
        (0.5 * courant) * ((low_flux[k] + high_flux[k]) - fastest * (high[k] - low[k]))
        for k in range(COMPS)
    ]


def interior_kernel(boxes, fine_ref, out_ref, speed_ref, pressure_ref, fast_ref):
    columns = FLAT // LANES
    row = iota((EDGE, LANES), 0)
    lane = iota((EDGE, LANES), 1)

    def column(step, _):
        box = step // columns
        at = pl.ds(pl.multiple_of((step % columns) * LANES, LANES), LANES)
        cells = [fine_ref[box, k, :, at] for k in range(COMPS)]
        inverse, pressure, sound = primitives(cells)
        speed_y = cells[2] * inverse
        speed_ref[:, pl.ds(pl.multiple_of(step * LANES, LANES), LANES)] = speed_y
        pressure_ref[:, pl.ds(pl.multiple_of(step * LANES, LANES), LANES)] = pressure
        fast_ref[:, pl.ds(pl.multiple_of(step * LANES, LANES), LANES)] = jnp.abs(speed_y) + sound
        total = list(cells)
        for normal, axis, keep in ((1, 0, row < EDGE - 1), (3, 1, lane % EDGE < EDGE - 1)):
            speed = cells[normal] * inverse
            state = (speed, pressure, jnp.abs(speed) + sound)
            ahead = [roll(c, -1, axis) for c in cells]
            ahead_state = [roll(c, -1, axis) for c in state]
            flux = scaled_flux(cells, ahead, normal, state, ahead_state)
            for k in range(COMPS):
                upper = jnp.where(keep, flux[k], 0.0)
                total[k] = total[k] - (upper - roll(upper, 1, axis))
        for k in range(COMPS):
            out_ref[box, k, :, at] = total[k]
        return 0

    lax.fori_loop(0, boxes * columns, column, 0)
    wide = iota((8, FLAT), 1)

    def rows(step, _):
        box = step // 4
        at = pl.ds(pl.multiple_of((step % 4) * 8, 8), 8)
        along = pl.ds(pl.multiple_of(box * FLAT, FLAT), FLAT)
        cells = [fine_ref[box, k, at, :] for k in range(COMPS)]
        state = [ref[at, along] for ref in (speed_ref, pressure_ref, fast_ref)]
        ahead = [roll(c, -EDGE, 1) for c in cells]
        ahead_state = [roll(c, -EDGE, 1) for c in state]
        flux = scaled_flux(cells, ahead, 2, state, ahead_state)
        for k in range(COMPS):
            upper = jnp.where(wide < FLAT - EDGE, flux[k], 0.0)
            out_ref[box, k, at, :] = out_ref[box, k, at, :] - (upper - roll(upper, EDGE, 1))
        return 0

    lax.fori_loop(0, boxes * 4, rows, 0)


def reply_kernel(code_ref, table_ref, out_ref, codes, sem):
    slots = out_ref.shape[0]
    rows = table_ref.shape[0]
    copy = pltpu.make_async_copy(code_ref, codes, sem)
    copy.start()
    copy.wait()

    def slot(i, _):
        code = codes[i, 0]

        @pl.when(code > 0)
        def _():
            out_ref[i] = table_ref[jnp.clip(code - 1, 0, rows - 1)]

        return 0

    lax.fori_loop(0, slots, slot, 0)


def boundary_kernel(
    boxes,
    blocks,
    line_size,
    fine_ids,
    coarse_ids,
    partial_ref,
    table_ref,
    replies_ref,
    out_ref,
    coarse_ref,
    flux_ref,
    pair_ref,
):
    for side in range(6):
        normal = side // 2 + 1

        def face_flux(box, _, side=side, normal=normal):
            face = box * 6 + side
            peer, _ = face_source(fine_ids, coarse_ids, box, side, boxes, blocks, line_size)
            own = [table_ref[face, 8 * k : 8 * k + 8, :] for k in range(COMPS)]
            ghost = [replies_ref[peer, 8 * k : 8 * k + 8, :] for k in range(COMPS)]
            states = []
            for cells in (own, ghost):
                inverse, pressure, sound = primitives(cells)
                speed = cells[normal] * inverse
                states.append((speed, pressure, jnp.abs(speed) + sound))
            if side % 2 == 0:
                flux = scaled_flux(ghost, own, normal, states[1], states[0])
            else:
                flux = scaled_flux(own, ghost, normal, states[0], states[1])
            for k in range(COMPS):
                flux_ref[face, 8 * k : 8 * k + 8, :] = flux[k]
            return 0

        lax.fori_loop(0, boxes, face_flux, 0)

    row = iota((8, LANES), 0)
    lane = iota((8, LANES), 1)
    inner = lane % 32
    row16 = iota((HALF, LANES), 0)
    lane16 = iota((HALF, LANES), 1)
    pick = 64 * ((lane16 // HALF) % 2) + 2 * (lane16 % HALF)

    def plane(step, _):
        box = step // COMPS
        comp = step % COMPS
        at = pl.ds(pl.multiple_of(comp * 8, 8), 8)
        faces = [flux_ref[box * 6 + side, at, :] for side in range(6)]
        for q in range(4):
            for v in range(8):
                spot = (box, comp, slice(8 * q, 8 * q + 8), slice(LANES * v, LANES * v + LANES))
                cells = partial_ref[spot]
                shift = 8 * q + v
                cells = cells + jnp.where(inner == 0, roll(faces[4], -shift, 1), 0.0)
                cells = cells - jnp.where(inner == 31, roll(faces[5], 31 - shift, 1), 0.0)
                if v == 0:
                    cells = cells + jnp.where(lane < 32, roll(faces[2], -32 * q, 1), 0.0)
                if v == 7:
                    cells = cells - jnp.where(lane >= 96, roll(faces[3], 96 - 32 * q, 1), 0.0)
                if q == 0:
                    cells = cells + jnp.where(row == 0, faces[0][v : v + 1], 0.0)
                if q == 3:
                    cells = cells - jnp.where(row == 7, faces[1][v : v + 1], 0.0)
                out_ref[spot] = cells
                pair_ref[v, 8 * q : 8 * q + 8, :] = cells
        for h in range(2):
            total = jnp.zeros((HALF, LANES), jnp.float32)
            for w in range(4):
                v = 4 * h + w
                pair = (
                    pair_ref[v, pl.ds(0, HALF, stride=2), :]
                    + pair_ref[v, pl.ds(1, HALF, stride=2), :]
                )
                pair = pair + roll(pair, -EDGE, 1)
                pair = pair + roll(pair, -1, 1)
                total = jnp.where(lane16 // 32 == w, lane_gather(pair, pick), total)
            coarse_ref[box, comp, :, LANES * h : LANES * h + LANES] = 0.125 * total
        return 0

    lax.fori_loop(0, boxes * COMPS, plane, 0)


def place_kernel(boxes, line_size, ring, covering_ref, coarse_ref, *rest):
    sources, out_ref = rest[:ring], rest[ring]
    me = lax.axis_index("gx")

    def block(i, _):
        box = covering_ref[i]
        column = lax.div(lax.div(box, boxes), line_size)
        away = lax.rem(column - me + ring, ring)
        slot = jnp.clip(lax.rem(box, boxes), 0, boxes - 1)

        @pl.when(box < 0)
        def _():
            out_ref[i] = coarse_ref[i]

        for k in range(ring):

            @pl.when((box >= 0) & (away == k))
            def _(k=k):
                out_ref[i] = sources[k][slot]

        return 0

    lax.fori_loop(0, out_ref.shape[0], block, 0)


def smem_spec():
    return pl.BlockSpec(memory_space=pltpu.SMEM)


def vmem_spec():
    return pl.BlockSpec(memory_space=pltpu.VMEM)


def near(x):
    return pltpu.with_memory_space_constraint(x, pltpu.VMEM)


def exchange(x):
    return lax.all_to_all(x, PLANE, split_axis=0, concat_axis=0, tiled=True)


def body(fine_state, coarse_state, neighbours, coarse_sources, covering):
    boxes = fine_state.shape[0]
    blocks = coarse_state.shape[0]
    line_size = lax.axis_size("gy") * lax.axis_size("gz")
    ring = lax.axis_size("gx")
    f32 = jnp.float32

    requests = pl.pallas_call(
        functools.partial(request_kernel, boxes, blocks, line_size),
        out_shape=jax.ShapeDtypeStruct((line_size, LANES), jnp.int32),
        in_specs=[smem_spec(), smem_spec()],
        out_specs=vmem_spec(),
        name="requests",
    )(neighbours, coarse_sources)
    codes = exchange(requests)

    table = pl.pallas_call(
        functools.partial(table_kernel, boxes, blocks),
        out_shape=pltpu.VMEM((6 * (boxes + blocks), SLOT_ROWS, LANES), f32),
        in_specs=[vmem_spec(), vmem_spec()],
        out_specs=vmem_spec(),
        name="tables",
    )(fine_state, coarse_state)

    partial = pl.pallas_call(
        functools.partial(interior_kernel, boxes),
        out_shape=pltpu.VMEM(fine_state.shape, f32),
        in_specs=[vmem_spec()],
        out_specs=vmem_spec(),
        scratch_shapes=[pltpu.VMEM((EDGE, boxes * FLAT), f32)] * 3,
        name="interior",
    )(fine_state)

    answers = pl.pallas_call(
        reply_kernel,
        out_shape=pltpu.VMEM((line_size, SLOT_ROWS, LANES), f32),
        in_specs=[vmem_spec(), vmem_spec()],
        out_specs=vmem_spec(),
        scratch_shapes=[pltpu.SMEM((line_size, LANES), jnp.int32), pltpu.SemaphoreType.DMA],
        name="answers",
    )(near(codes), near(table))
    replies = exchange(answers)

    fine_next, restricted = pl.pallas_call(
        functools.partial(boundary_kernel, boxes, blocks, line_size),
        out_shape=(
            jax.ShapeDtypeStruct(fine_state.shape, f32),
            pltpu.VMEM((boxes, COMPS, HALF, SMALL), f32),
        ),
        in_specs=[smem_spec(), smem_spec(), vmem_spec(), vmem_spec(), vmem_spec()],
        out_specs=(vmem_spec(), vmem_spec()),
        scratch_shapes=[
            pltpu.VMEM((6 * boxes, SLOT_ROWS, LANES), f32),
            pltpu.VMEM((8, EDGE, LANES), f32),
        ],
        name="boundary",
    )(neighbours, coarse_sources, near(partial), near(table), near(replies))

    def shift(x, step):
        return lax.ppermute(x, "gx", [(i, (i + step) % ring) for i in range(ring)])

    gathered = {0: restricted}
    right = left = restricted
    for hop in range(1, ring // 2 + 1):
        right = shift(right, 1)
        gathered[ring - hop] = right
        if hop < ring - hop:
            left = shift(left, -1)
            gathered[hop] = left

    coarse_next = pl.pallas_call(
        functools.partial(place_kernel, boxes, line_size, ring),
        out_shape=jax.ShapeDtypeStruct(coarse_state.shape, f32),
        in_specs=[smem_spec()] + [vmem_spec()] * (ring + 1),
        out_specs=vmem_spec(),
        name="place",
    )(covering, coarse_state, *[near(gathered[k]) for k in range(ring)])
    return fine_next, coarse_next


def solution(mesh):
    spec = P(AXES)
    return jax.shard_map(
        body, mesh=mesh, in_specs=(spec,) * 5, out_specs=(spec, spec), check_vma=False
    )
```

```python
import functools

import jax
import jax.numpy as jnp
from jax import lax
from jax.experimental import pallas as pl
from jax.experimental.pallas import tpu as pltpu
from jax.sharding import PartitionSpec as P

adiabatic = 5.0 / 3.0
courant = 0.12
AXES = ("gx", "gy", "gz")
PLANE = ("gy", "gz")

EDGE = 32
HALF = 16
FLAT = EDGE * EDGE
SMALL = HALF * HALF
LANES = 128
COMPS = 5
SLOT_ROWS = COMPS * FLAT // LANES


def iota(shape, dim):
    return lax.broadcasted_iota(jnp.int32, shape, dim)


def roll(x, shift, axis):
    size = x.shape[axis]
    shift = shift % size
    return x if shift == 0 else pltpu.roll(x, shift, axis)


def quotient(x, n):
    return lax.shift_right_logical(x, n.bit_length() - 1) if n & (n - 1) == 0 else lax.div(x, n)


def remainder(x, n):
    return lax.bitwise_and(x, n - 1) if n & (n - 1) == 0 else lax.rem(x, n)


def face_source(fine_ref, coarse_ref, box, side, boxes, blocks, line_size):
    fine_id = fine_ref[box, side]
    coarse_id = coarse_ref[box, side]
    is_fine = fine_id >= 0
    device = jnp.where(is_fine, quotient(fine_id, boxes), quotient(coarse_id, blocks))
    row = jnp.where(
        is_fine,
        remainder(fine_id, boxes) * 6 + (side ^ 1),
        boxes * 6 + remainder(coarse_id, blocks) * 6 + (side ^ 1),
    )
    return remainder(device, line_size), row


def request_kernel(boxes, blocks, line_size, fine_ref, coarse_ref, out_ref):
    peers = iota(out_ref.shape, 0)
    table = jnp.zeros(out_ref.shape, jnp.int32)
    for box in range(boxes):
        for side in range(6):
            peer, row = face_source(fine_ref, coarse_ref, box, side, boxes, blocks, line_size)
            table = jnp.where(peers == peer, row + 1, table)
    out_ref[...] = table


def lane_gather(x, index):
    return jnp.take_along_axis(x, index, axis=1)


def row_gather(x, index):
    return jnp.take_along_axis(x, index, axis=0)


def table_kernel(boxes, blocks, fine_ref, coarse_ref, out_ref):
    row = iota((8, LANES), 0)
    lane = iota((8, LANES), 1)
    quad = lane // 32
    inner = lane % 32

    def fine_box(box, _):
        base = box * 6
        for comp in range(COMPS):
            dst = slice(8 * comp, 8 * comp + 8)
            for side, first in ((0, 0), (1, EDGE - 1)):
                for r in range(8):
                    out_ref[base + side, 8 * comp + r : 8 * comp + r + 1, :] = fine_ref[
                        box, comp, first : first + 1, LANES * r : LANES * r + LANES
                    ]
            y_low = jnp.zeros((8, LANES), jnp.float32)
            y_high = y_low
            z_low = y_low
            z_high = y_low
            for q in range(4):
                for v in range(8):
                    cells = fine_ref[box, comp, 8 * q : 8 * q + 8, LANES * v : LANES * v + LANES]
                    if v == 0:
                        y_low = jnp.where(quad == q, roll(cells, 32 * q, 1), y_low)
                    if v == 7:
                        y_high = jnp.where(quad == q, roll(cells, 32 * q - 96, 1), y_high)
                    spot = inner == 8 * q + v
                    z_low = jnp.where(spot, roll(cells, 8 * q + v, 1), z_low)
                    z_high = jnp.where(spot, roll(cells, 8 * q + v - 31, 1), z_high)
            out_ref[base + 2, dst, :] = y_low
            out_ref[base + 3, dst, :] = y_high
            out_ref[base + 4, dst, :] = z_low
            out_ref[base + 5, dst, :] = z_high
        return 0

    lax.fori_loop(0, boxes, fine_box, 0)

    pick_x = 32 * (row % 4) + 16 * (quad // 2) + inner // 2
    pick_y = inner // 2
    pick_z = 32 * (inner % 4) + 16 * (quad // 2)
    rows_y = 4 * (quad % 2) + row // 2
    rows_z = 4 * ((inner // 8) % 2) + row // 2

    def coarse_block(block, _):
        base = boxes * 6 + block * 6
        for comp in range(COMPS):
            dst = slice(8 * comp, 8 * comp + 8)
            cells = [
                [
                    coarse_ref[block, comp, 8 * g : 8 * g + 8, LANES * h : LANES * h + LANES]
                    for h in range(2)
                ]
                for g in range(2)
            ]
            for side, first in ((0, 0), (1, HALF - 1)):
                parts = [
                    jnp.broadcast_to(cells[first // 8][h][first % 8 : first % 8 + 1], (8, LANES))
                    for h in range(2)
                ]
                out_ref[base + side, dst, :] = jnp.where(
                    row < 4, lane_gather(parts[0], pick_x), lane_gather(parts[1], pick_x)
                )
            for side, half, start in ((2, 0, 0), (3, 1, LANES - HALF)):
                parts = [
                    row_gather(lane_gather(cells[g][half], pick_y + start), rows_y)
                    for g in range(2)
                ]
                out_ref[base + side, dst, :] = jnp.where(quad < 2, parts[0], parts[1])
            for side, last in ((4, 0), (5, HALF - 1)):
                parts = [
                    row_gather(
                        jnp.where(
                            inner % 8 < 4,
                            lane_gather(cells[g][0], pick_z + last),
                            lane_gather(cells[g][1], pick_z + last),
                        ),
                        rows_z,
                    )
                    for g in range(2)
                ]
                out_ref[base + side, dst, :] = jnp.where(inner < 16, parts[0], parts[1])
        return 0

    lax.fori_loop(0, blocks, coarse_block, 0)


def primitives(cells):
    inverse = 1.0 / cells[0]
    kinetic = (
        0.5 * (cells[1] * cells[1] + cells[2] * cells[2] + cells[3] * cells[3]) * inverse
    )
    pressure = (adiabatic - 1.0) * (cells[4] - kinetic)
    sound = jnp.sqrt(adiabatic * pressure * inverse)
    return inverse, pressure, sound


def physical_flux(cells, normal, speed, pressure):
    entries = [
        cells[normal],
        cells[1] * speed,
        cells[2] * speed,
        cells[3] * speed,
        (cells[4] + pressure) * speed,
    ]
    entries[normal] = entries[normal] + pressure
    return entries


def scaled_flux(low, high, normal, low_state, high_state):
    low_speed, low_pressure, low_fast = low_state
    high_speed, high_pressure, high_fast = high_state
    fastest = jnp.maximum(low_fast, high_fast)
    low_flux = physical_flux(low, normal, low_speed, low_pressure)
    high_flux = physical_flux(high, normal, high_speed, high_pressure)
    return [
        (0.5 * courant) * ((low_flux[k] + high_flux[k]) - fastest * (high[k] - low[k]))
        for k in range(COMPS)
    ]


def interior_kernel(
    boxes, fine_ref, out_ref, coarse_ref, speed_ref, pressure_ref, fast_ref, pair_ref
):
    columns = FLAT // LANES
    row = iota((EDGE, LANES), 0)
    lane = iota((EDGE, LANES), 1)

    def column(step, _):
        box = step // columns
        at = pl.ds(pl.multiple_of((step % columns) * LANES, LANES), LANES)
        cells = [fine_ref[box, k, :, at] for k in range(COMPS)]
        inverse, pressure, sound = primitives(cells)
        speed_y = cells[2] * inverse
        speed_ref[:, pl.ds(pl.multiple_of(step * LANES, LANES), LANES)] = speed_y
        pressure_ref[:, pl.ds(pl.multiple_of(step * LANES, LANES), LANES)] = pressure
        fast_ref[:, pl.ds(pl.multiple_of(step * LANES, LANES), LANES)] = jnp.abs(speed_y) + sound
        total = list(cells)
        for normal, axis, keep in ((1, 0, row < EDGE - 1), (3, 1, lane % EDGE < EDGE - 1)):
            speed = cells[normal] * inverse
            state = (speed, pressure, jnp.abs(speed) + sound)
            ahead = [roll(c, -1, axis) for c in cells]
            ahead_state = [roll(c, -1, axis) for c in state]
            flux = scaled_flux(cells, ahead, normal, state, ahead_state)
            for k in range(COMPS):
                upper = jnp.where(keep, flux[k], 0.0)
                total[k] = total[k] - (upper - roll(upper, 1, axis))
        for k in range(COMPS):
            out_ref[box, k, :, at] = total[k]
        return 0

    lax.fori_loop(0, boxes * columns, column, 0)
    wide = iota((8, FLAT), 1)

    def rows(step, _):
        box = step // 4
        at = pl.ds(pl.multiple_of((step % 4) * 8, 8), 8)
        along = pl.ds(pl.multiple_of(box * FLAT, FLAT), FLAT)
        cells = [fine_ref[box, k, at, :] for k in range(COMPS)]
        state = [ref[at, along] for ref in (speed_ref, pressure_ref, fast_ref)]
        ahead = [roll(c, -EDGE, 1) for c in cells]
        ahead_state = [roll(c, -EDGE, 1) for c in state]
        flux = scaled_flux(cells, ahead, 2, state, ahead_state)
        for k in range(COMPS):
            upper = jnp.where(wide < FLAT - EDGE, flux[k], 0.0)
            out_ref[box, k, at, :] = out_ref[box, k, at, :] - (upper - roll(upper, EDGE, 1))
        return 0

    lax.fori_loop(0, boxes * 4, rows, 0)
    lane16 = iota((HALF, LANES), 1)
    pick = 64 * ((lane16 // HALF) % 2) + 2 * (lane16 % HALF)

    def restrict(step, _):
        box = step // COMPS
        comp = step % COMPS
        for h in range(2):
            total = jnp.zeros((HALF, LANES), jnp.float32)
            for w in range(4):
                v = 4 * h + w
                pair_ref[v] = out_ref[box, comp, :, LANES * v : LANES * v + LANES]
                pair = (
                    pair_ref[v, pl.ds(0, HALF, stride=2), :]
                    + pair_ref[v, pl.ds(1, HALF, stride=2), :]
                )
                pair = pair + roll(pair, -EDGE, 1)
                pair = pair + roll(pair, -1, 1)
                total = jnp.where(lane16 // 32 == w, lane_gather(pair, pick), total)
            coarse_ref[box, comp, :, LANES * h : LANES * h + LANES] = 0.125 * total
        return 0

    lax.fori_loop(0, boxes * COMPS, restrict, 0)


def reply_kernel(code_ref, table_ref, out_ref, codes, sem, sems):
    slots = out_ref.shape[0]
    rows = table_ref.shape[0]
    copy = pltpu.make_async_copy(code_ref, codes, sem)
    copy.start()
    copy.wait()

    def each(act):
        for i in range(slots):
            code = codes[i, 0]

            @pl.when(code > 0)
            def _(i=i, code=code):
                source = table_ref.at[jnp.clip(code - 1, 0, rows - 1)]
                act(pltpu.make_async_copy(source, out_ref.at[i], sems.at[i]))

    each(lambda copy: copy.start())
    each(lambda copy: copy.wait())


def flux_kernel(
    boxes,
    blocks,
    line_size,
    fine_ids,
    coarse_ids,
    interior_ref,
    table_ref,
    replies_ref,
    flux_ref,
    coarse_ref,
):
    for face in range(6 * boxes):
        box, side = face // 6, face % 6
        normal = side // 2 + 1
        peer, _ = face_source(fine_ids, coarse_ids, box, side, boxes, blocks, line_size)
        own = [table_ref[face, 8 * k : 8 * k + 8, :] for k in range(COMPS)]
        ghost = [replies_ref[peer, 8 * k : 8 * k + 8, :] for k in range(COMPS)]
        states = []
        for cells in (own, ghost):
            inverse, pressure, sound = primitives(cells)
            speed = cells[normal] * inverse
            states.append((speed, pressure, jnp.abs(speed) + sound))
        if side % 2 == 0:
            flux = scaled_flux(ghost, own, normal, states[1], states[0])
        else:
            flux = scaled_flux(own, ghost, normal, states[0], states[1])
        for k in range(COMPS):
            flux_ref[face, 8 * k : 8 * k + 8, :] = flux[k]

    row = iota((8, LANES), 0)
    lane = iota((8, LANES), 1)
    even = 2 * (row % 4)

    def restrict(step, _):
        box = step // COMPS
        comp = step % COMPS
        at = pl.ds(pl.multiple_of(comp * 8, 8), 8)
        faces = [flux_ref[box * 6 + side, at, :] * (0.125 if side % 2 == 0 else -0.125) for side in range(6)]
        for side in range(6):
            face = faces[side]
            if side < 2:
                face = face + roll(face, -1, 1)
                face = face + roll(face, -EDGE, 1)
                face = lane_gather(face, 64 * ((lane // HALF) % 2) + 2 * (lane % HALF))
            else:
                face = face + roll(face, -1, 0)
                face = face + roll(face, -1 if side < 4 else -EDGE, 1)
                face = row_gather(face, even)
            faces[side] = face
        for t in range(2):
            quarter = 2 * t + row // 4
            for h in range(2):
                spot = (box, comp, slice(8 * t, 8 * t + 8), slice(LANES * h, LANES * h + LANES))
                cells = interior_ref[spot]
                pick = 64 * ((lane // HALF) % 2) + 8 * quarter + 4 * h + lane // 32
                cells = cells + jnp.where(lane % HALF == 0, lane_gather(faces[4], pick), 0.0)
                cells = cells + jnp.where(
                    lane % HALF == HALF - 1, lane_gather(faces[5], pick), 0.0
                )
                pick = 32 * quarter + 2 * (lane % HALF)
                near_edge = lane < HALF if h == 0 else lane >= LANES - HALF
                cells = cells + jnp.where(near_edge, lane_gather(faces[2 + h], pick), 0.0)
                first = row == 0 if t == 0 else row == 7
                cells = cells + jnp.where(first, row_gather(faces[t], 4 * h + lane // 32), 0.0)
                coarse_ref[spot] = cells
        return 0

    lax.fori_loop(0, boxes * COMPS, restrict, 0)


def finish_kernel(boxes, partial_ref, flux_ref, out_ref):
    row = iota((8, LANES), 0)
    lane = iota((8, LANES), 1)
    inner = lane % 32

    def plane(step, _):
        box = step // COMPS
        comp = step % COMPS
        at = pl.ds(pl.multiple_of(comp * 8, 8), 8)
        faces = [flux_ref[box * 6 + side, at, :] for side in range(6)]
        for q in range(4):
            for v in range(8):
                spot = (box, comp, slice(8 * q, 8 * q + 8), slice(LANES * v, LANES * v + LANES))
                cells = partial_ref[spot]
                shift = 8 * q + v
                cells = cells + jnp.where(inner == 0, roll(faces[4], -shift, 1), 0.0)
                cells = cells - jnp.where(inner == 31, roll(faces[5], 31 - shift, 1), 0.0)
                if v == 0:
                    cells = cells + jnp.where(lane < 32, roll(faces[2], -32 * q, 1), 0.0)
                if v == 7:
                    cells = cells - jnp.where(lane >= 96, roll(faces[3], 96 - 32 * q, 1), 0.0)
                if q == 0:
                    cells = cells + jnp.where(row == 0, faces[0][v : v + 1], 0.0)
                if q == 3:
                    cells = cells - jnp.where(row == 7, faces[1][v : v + 1], 0.0)
                out_ref[spot] = cells
        return 0

    lax.fori_loop(0, boxes * COMPS, plane, 0)


def copy_kernel(x_ref, out_ref):
    out_ref[...] = x_ref[...]


def place_kernel(boxes, line_size, ring, covering_ref, _, *rest):
    sources = rest[:ring]
    out_ref, sems = rest[ring], rest[ring + 1]
    me = lax.axis_index("gx")

    def each(act):
        for i in range(out_ref.shape[0]):
            box = covering_ref[i]
            column = quotient(quotient(box, boxes), line_size)
            away = remainder(column - me + ring, ring)
            slot = jnp.clip(remainder(box, boxes), 0, boxes - 1)

            for k in range(ring):

                @pl.when((box >= 0) & (away == k))
                def _(i=i, k=k, slot=slot):
                    act(pltpu.make_async_copy(sources[k].at[slot], out_ref.at[i], sems.at[i]))

    each(lambda copy: copy.start())

    def finish(i, _):
        @pl.when(covering_ref[i] >= 0)
        def _():
            pltpu.make_async_copy(sources[0].at[0], out_ref.at[i], sems.at[i]).wait()

        return 0

    lax.fori_loop(0, out_ref.shape[0], finish, 0)


def any_spec():
    return pl.BlockSpec(memory_space=pl.ANY)


def smem_spec():
    return pl.BlockSpec(memory_space=pltpu.SMEM)


def vmem_spec():
    return pl.BlockSpec(memory_space=pltpu.VMEM)


def kernel_params(mib=16):
    return pltpu.CompilerParams(vmem_limit_bytes=mib << 20)


def near(x):
    return pltpu.with_memory_space_constraint(x, pltpu.VMEM)


def far(x):
    return pltpu.with_memory_space_constraint(x, pltpu.HBM)


def exchange(x):
    return lax.all_to_all(x, PLANE, split_axis=0, concat_axis=0, tiled=True)


def body(fine_state, coarse_state, neighbours, coarse_sources, covering):
    boxes = fine_state.shape[0]
    blocks = coarse_state.shape[0]
    line_size = lax.axis_size("gy") * lax.axis_size("gz")
    ring = lax.axis_size("gx")
    f32 = jnp.float32

    requests = pl.pallas_call(
        functools.partial(request_kernel, boxes, blocks, line_size),
        out_shape=jax.ShapeDtypeStruct((line_size, LANES), jnp.int32),
        in_specs=[smem_spec(), smem_spec()],
        out_specs=vmem_spec(),
        name="requests",
    )(far(neighbours), far(coarse_sources))
    codes = exchange(requests)

    table = pl.pallas_call(
        functools.partial(table_kernel, boxes, blocks),
        out_shape=pltpu.VMEM((6 * (boxes + blocks), SLOT_ROWS, LANES), f32),
        in_specs=[vmem_spec(), vmem_spec()],
        out_specs=vmem_spec(),
        compiler_params=kernel_params(),
        name="tables",
    )(fine_state, coarse_state)

    partial, interior = pl.pallas_call(
        functools.partial(interior_kernel, boxes),
        out_shape=(
            pltpu.VMEM(fine_state.shape, f32),
            pltpu.VMEM((boxes, COMPS, HALF, SMALL), f32),
        ),
        in_specs=[vmem_spec()],
        out_specs=(vmem_spec(), vmem_spec()),
        scratch_shapes=[pltpu.VMEM((EDGE, boxes * FLAT), f32)] * 3
        + [pltpu.VMEM((8, EDGE, LANES), f32)],
        compiler_params=kernel_params(),
        name="interior",
    )(fine_state)

    answers = pl.pallas_call(
        reply_kernel,
        out_shape=pltpu.HBM((line_size, SLOT_ROWS, LANES), f32),
        in_specs=[vmem_spec(), vmem_spec()],
        out_specs=pl.BlockSpec(memory_space=pltpu.HBM),
        scratch_shapes=[
            pltpu.SMEM((line_size, LANES), jnp.int32),
            pltpu.SemaphoreType.DMA,
            pltpu.SemaphoreType.DMA((line_size,)),
        ],
        compiler_params=kernel_params(),
        name="answers",
    )(near(codes), near(table))
    replies = exchange(answers)

    flux, restricted = pl.pallas_call(
        functools.partial(flux_kernel, boxes, blocks, line_size),
        out_shape=(
            pltpu.VMEM((6 * boxes, SLOT_ROWS, LANES), f32),
            pltpu.VMEM((boxes, COMPS, HALF, SMALL), f32),
        ),
        in_specs=[smem_spec(), smem_spec(), vmem_spec(), vmem_spec(), vmem_spec()],
        out_specs=(vmem_spec(), vmem_spec()),
        compiler_params=kernel_params(),
        name="fluxes",
    )(far(neighbours), far(coarse_sources), near(interior), near(table), near(replies))

    fine_next = pl.pallas_call(
        functools.partial(finish_kernel, boxes),
        out_shape=jax.ShapeDtypeStruct(fine_state.shape, f32),
        in_specs=[vmem_spec(), vmem_spec()],
        out_specs=vmem_spec(),
        compiler_params=kernel_params(),
        name="finish",
    )(near(partial), near(flux))

    prior = pl.pallas_call(
        copy_kernel,
        out_shape=jax.ShapeDtypeStruct(coarse_state.shape, f32),
        in_specs=[vmem_spec()],
        out_specs=vmem_spec(),
        compiler_params=kernel_params(),
        name="prior",
    )(coarse_state)

    def shift(x, step):
        return lax.ppermute(x, "gx", [(i, (i + step) % ring) for i in range(ring)])

    gathered = {0: restricted}
    right = left = restricted
    for hop in range(1, ring // 2 + 1):
        right = shift(right, 1)
        gathered[ring - hop] = right
        if hop < ring - hop:
            left = shift(left, -1)
            gathered[hop] = left

    coarse_next = pl.pallas_call(
        functools.partial(place_kernel, boxes, line_size, ring),
        out_shape=jax.ShapeDtypeStruct(coarse_state.shape, f32),
        in_specs=[smem_spec(), any_spec()] + [vmem_spec()] * ring,
        out_specs=any_spec(),
        scratch_shapes=[pltpu.SemaphoreType.DMA((blocks,))],
        input_output_aliases={1: 0},
        compiler_params=kernel_params(),
        name="place",
    )(far(covering), prior, *[near(gathered[k]) for k in range(ring)])
    return fine_next, coarse_next


def solution(mesh):
    spec = P(AXES)
    return jax.shard_map(
        body, mesh=mesh, in_specs=(spec,) * 5, out_specs=(spec, spec), check_vma=False
    )
```

```python
import functools

import jax
import jax.numpy as jnp
from jax import lax
from jax.experimental import pallas as pl
from jax.experimental.pallas import tpu as pltpu
from jax.sharding import PartitionSpec as P

adiabatic = 5.0 / 3.0
courant = 0.12
AXES = ("gx", "gy", "gz")
PLANE = ("gy", "gz")

EDGE = 32
HALF = 16
FLAT = EDGE * EDGE
SMALL = HALF * HALF
LANES = 128
COMPS = 5
SLOT_ROWS = COMPS * FLAT // LANES


def iota(shape, dim):
    return lax.broadcasted_iota(jnp.int32, shape, dim)


def roll(x, shift, axis):
    size = x.shape[axis]
    shift = shift % size
    return x if shift == 0 else pltpu.roll(x, shift, axis)


def quotient(x, n):
    return lax.shift_right_logical(x, n.bit_length() - 1) if n & (n - 1) == 0 else lax.div(x, n)


def remainder(x, n):
    return lax.bitwise_and(x, n - 1) if n & (n - 1) == 0 else lax.rem(x, n)


def face_source(fine_ref, coarse_ref, box, side, boxes, blocks, line_size):
    fine_id = fine_ref[box, side]
    coarse_id = coarse_ref[box, side]
    is_fine = fine_id >= 0
    device = jnp.where(is_fine, quotient(fine_id, boxes), quotient(coarse_id, blocks))
    row = jnp.where(
        is_fine,
        remainder(fine_id, boxes) * 6 + (side ^ 1),
        boxes * 6 + remainder(coarse_id, blocks) * 6 + (side ^ 1),
    )
    return remainder(device, line_size), row


def request_kernel(
    boxes, blocks, line_size, fine_ref, coarse_ref, covering_ref, out_ref, wants_ref
):
    peers = iota(out_ref.shape, 0)
    table = jnp.zeros(out_ref.shape, jnp.int32)
    for box in range(boxes):
        for side in range(6):
            peer, row = face_source(fine_ref, coarse_ref, box, side, boxes, blocks, line_size)
            table = jnp.where(peers == peer, row + 1, table)
    out_ref[...] = table
    column = jnp.where(
        iota(wants_ref.shape, 0) == lax.axis_index("gx"), iota(wants_ref.shape, 1), -1
    )
    wants = jnp.zeros(wants_ref.shape, jnp.int32)
    for i in range(blocks):
        box = covering_ref[i]
        owner = jnp.where(box >= 0, quotient(quotient(box, boxes), line_size), -2)
        wants = jnp.where(column == owner, remainder(box, boxes) + 1, wants)
    wants_ref[...] = wants


def lane_gather(x, index):
    return jnp.take_along_axis(x, index, axis=1)


def row_gather(x, index):
    return jnp.take_along_axis(x, index, axis=0)


def table_kernel(boxes, blocks, fine_ref, coarse_ref, out_ref):
    row = iota((8, LANES), 0)
    lane = iota((8, LANES), 1)
    quad = lane // 32
    inner = lane % 32

    def fine_box(box, _):
        base = box * 6
        for comp in range(COMPS):
            dst = slice(8 * comp, 8 * comp + 8)
            for side, first in ((0, 0), (1, EDGE - 1)):
                for r in range(8):
                    out_ref[base + side, 8 * comp + r : 8 * comp + r + 1, :] = fine_ref[
                        box, comp, first : first + 1, LANES * r : LANES * r + LANES
                    ]
            y_low = jnp.zeros((8, LANES), jnp.float32)
            y_high = y_low
            z_low = y_low
            z_high = y_low
            for q in range(4):
                for v in range(8):
                    cells = fine_ref[box, comp, 8 * q : 8 * q + 8, LANES * v : LANES * v + LANES]
                    if v == 0:
                        y_low = jnp.where(quad == q, roll(cells, 32 * q, 1), y_low)
                    if v == 7:
                        y_high = jnp.where(quad == q, roll(cells, 32 * q - 96, 1), y_high)
                    spot = inner == 8 * q + v
                    z_low = jnp.where(spot, roll(cells, 8 * q + v, 1), z_low)
                    z_high = jnp.where(spot, roll(cells, 8 * q + v - 31, 1), z_high)
            out_ref[base + 2, dst, :] = y_low
            out_ref[base + 3, dst, :] = y_high
            out_ref[base + 4, dst, :] = z_low
            out_ref[base + 5, dst, :] = z_high
        return 0

    lax.fori_loop(0, boxes, fine_box, 0)

    pick_x = 32 * (row % 4) + 16 * (quad // 2) + inner // 2
    pick_y = inner // 2
    pick_z = 32 * (inner % 4) + 16 * (quad // 2)
    rows_y = 4 * (quad % 2) + row // 2
    rows_z = 4 * ((inner // 8) % 2) + row // 2

    def coarse_block(block, _):
        base = boxes * 6 + block * 6
        for comp in range(COMPS):
            dst = slice(8 * comp, 8 * comp + 8)
            cells = [
                [
                    coarse_ref[block, comp, 8 * g : 8 * g + 8, LANES * h : LANES * h + LANES]
                    for h in range(2)
                ]
                for g in range(2)
            ]
            for side, first in ((0, 0), (1, HALF - 1)):
                parts = [
                    jnp.broadcast_to(cells[first // 8][h][first % 8 : first % 8 + 1], (8, LANES))
                    for h in range(2)
                ]
                out_ref[base + side, dst, :] = jnp.where(
                    row < 4, lane_gather(parts[0], pick_x), lane_gather(parts[1], pick_x)
                )
            for side, half, start in ((2, 0, 0), (3, 1, LANES - HALF)):
                parts = [
                    row_gather(lane_gather(cells[g][half], pick_y + start), rows_y)
                    for g in range(2)
                ]
                out_ref[base + side, dst, :] = jnp.where(quad < 2, parts[0], parts[1])
            for side, last in ((4, 0), (5, HALF - 1)):
                parts = [
                    row_gather(
                        jnp.where(
                            inner % 8 < 4,
                            lane_gather(cells[g][0], pick_z + last),
                            lane_gather(cells[g][1], pick_z + last),
                        ),
                        rows_z,
                    )
                    for g in range(2)
                ]
                out_ref[base + side, dst, :] = jnp.where(inner < 16, parts[0], parts[1])
        return 0

    lax.fori_loop(0, blocks, coarse_block, 0)


def primitives(cells):
    inverse = 1.0 / cells[0]
    kinetic = (
        0.5 * (cells[1] * cells[1] + cells[2] * cells[2] + cells[3] * cells[3]) * inverse
    )
    pressure = (adiabatic - 1.0) * (cells[4] - kinetic)
    sound = jnp.sqrt(adiabatic * pressure * inverse)
    return inverse, pressure, sound


def physical_flux(cells, normal, speed, pressure):
    entries = [
        cells[normal],
        cells[1] * speed,
        cells[2] * speed,
        cells[3] * speed,
        (cells[4] + pressure) * speed,
    ]
    entries[normal] = entries[normal] + pressure
    return entries


def scaled_flux(low, high, normal, low_state, high_state):
    low_speed, low_pressure, low_fast = low_state
    high_speed, high_pressure, high_fast = high_state
    fastest = jnp.maximum(low_fast, high_fast)
    low_flux = physical_flux(low, normal, low_speed, low_pressure)
    high_flux = physical_flux(high, normal, high_speed, high_pressure)
    return [
        (0.5 * courant) * ((low_flux[k] + high_flux[k]) - fastest * (high[k] - low[k]))
        for k in range(COMPS)
    ]


def interior_kernel(
    boxes,
    fine_ref,
    wants_a,
    wants_b,
    partial_ref,
    restricted_ref,
    wants_ref,
    out_ref,
    coarse_ref,
    speed_ref,
    pressure_ref,
    fast_ref,
    pair_ref,
    sems,
):
    wants_ref[...] = wants_a[...] + wants_b[...]
    columns = FLAT // LANES
    row = iota((EDGE, LANES), 0)
    lane = iota((EDGE, LANES), 1)

    def column(step, _):
        box = step // columns
        at = pl.ds(pl.multiple_of((step % columns) * LANES, LANES), LANES)
        cells = [fine_ref[box, k, :, at] for k in range(COMPS)]
        inverse, pressure, sound = primitives(cells)
        speed_y = cells[2] * inverse
        speed_ref[:, pl.ds(pl.multiple_of(step * LANES, LANES), LANES)] = speed_y
        pressure_ref[:, pl.ds(pl.multiple_of(step * LANES, LANES), LANES)] = pressure
        fast_ref[:, pl.ds(pl.multiple_of(step * LANES, LANES), LANES)] = jnp.abs(speed_y) + sound
        total = list(cells)
        for normal, axis, keep in ((1, 0, row < EDGE - 1), (3, 1, lane % EDGE < EDGE - 1)):
            speed = cells[normal] * inverse
            state = (speed, pressure, jnp.abs(speed) + sound)
            ahead = [roll(c, -1, axis) for c in cells]
            ahead_state = [roll(c, -1, axis) for c in state]
            flux = scaled_flux(cells, ahead, normal, state, ahead_state)
            for k in range(COMPS):
                upper = jnp.where(keep, flux[k], 0.0)
                total[k] = total[k] - (upper - roll(upper, 1, axis))
        for k in range(COMPS):
            out_ref[box, k, :, at] = total[k]
        return 0

    lax.fori_loop(0, boxes * columns, column, 0)
    wide = iota((8, FLAT), 1)

    def rows(step, _):
        box = step // 4
        at = pl.ds(pl.multiple_of((step % 4) * 8, 8), 8)
        along = pl.ds(pl.multiple_of(box * FLAT, FLAT), FLAT)
        cells = [fine_ref[box, k, at, :] for k in range(COMPS)]
        state = [ref[at, along] for ref in (speed_ref, pressure_ref, fast_ref)]
        ahead = [roll(c, -EDGE, 1) for c in cells]
        ahead_state = [roll(c, -EDGE, 1) for c in state]
        flux = scaled_flux(cells, ahead, 2, state, ahead_state)
        for k in range(COMPS):
            upper = jnp.where(wide < FLAT - EDGE, flux[k], 0.0)
            out_ref[box, k, at, :] = out_ref[box, k, at, :] - (upper - roll(upper, EDGE, 1))
        return 0

    lax.fori_loop(0, boxes * 4, rows, 0)
    save = pltpu.make_async_copy(out_ref, partial_ref, sems.at[0])
    save.start()
    lane16 = iota((HALF, LANES), 1)
    pick = 64 * ((lane16 // HALF) % 2) + 2 * (lane16 % HALF)

    def restrict(step, _):
        box = step // COMPS
        comp = step % COMPS
        for h in range(2):
            total = jnp.zeros((HALF, LANES), jnp.float32)
            for w in range(4):
                v = 4 * h + w
                pair_ref[v] = out_ref[box, comp, :, LANES * v : LANES * v + LANES]
                pair = (
                    pair_ref[v, pl.ds(0, HALF, stride=2), :]
                    + pair_ref[v, pl.ds(1, HALF, stride=2), :]
                )
                pair = pair + roll(pair, -EDGE, 1)
                pair = pair + roll(pair, -1, 1)
                total = jnp.where(lane16 // 32 == w, lane_gather(pair, pick), total)
            coarse_ref[box, comp, :, LANES * h : LANES * h + LANES] = 0.125 * total
        return 0

    lax.fori_loop(0, boxes * COMPS, restrict, 0)
    last = pltpu.make_async_copy(coarse_ref, restricted_ref, sems.at[1])
    last.start()
    save.wait()
    last.wait()


def reply_kernel(code_ref, table_ref, wants_a, wants_b, out_ref, wants_ref, codes, sem, sems):
    slots = out_ref.shape[0]
    rows = table_ref.shape[0]
    copy = pltpu.make_async_copy(code_ref, codes, sem)
    copy.start()
    copy.wait()

    def each(act):
        for i in range(slots):
            code = codes[i, 0]

            @pl.when(code > 0)
            def _(i=i, code=code):
                source = table_ref.at[jnp.clip(code - 1, 0, rows - 1)]
                act(pltpu.make_async_copy(source, out_ref.at[i], sems.at[i]))

    each(lambda copy: copy.start())
    wants_ref[...] = wants_a[...] + wants_b[...]
    each(lambda copy: copy.wait())


def flux_kernel(
    boxes,
    blocks,
    line_size,
    fine_ids,
    coarse_ids,
    restricted_ref,
    table_ref,
    replies_ref,
    wants_a,
    wants_b,
    flux_ref,
    send_ref,
    interior_ref,
    coarse_ref,
    wants_ref,
    wanted,
    fetch_sems,
    sems,
):
    me = lax.axis_index("gx")
    wants_ref[...] = wants_a[...] + wants_b[...]
    fetches = [
        pltpu.make_async_copy(wants_ref, wanted, fetch_sems.at[0]),
        pltpu.make_async_copy(restricted_ref, interior_ref, fetch_sems.at[1]),
    ]
    for fetch in fetches:
        fetch.start()
    for face in range(6 * boxes):
        box, side = face // 6, face % 6
        normal = side // 2 + 1
        peer, _ = face_source(fine_ids, coarse_ids, box, side, boxes, blocks, line_size)
        own = [table_ref[face, 8 * k : 8 * k + 8, :] for k in range(COMPS)]
        ghost = [replies_ref[peer, 8 * k : 8 * k + 8, :] for k in range(COMPS)]
        states = []
        for cells in (own, ghost):
            inverse, pressure, sound = primitives(cells)
            speed = cells[normal] * inverse
            states.append((speed, pressure, jnp.abs(speed) + sound))
        if side % 2 == 0:
            flux = scaled_flux(ghost, own, normal, states[1], states[0])
        else:
            flux = scaled_flux(own, ghost, normal, states[0], states[1])
        for k in range(COMPS):
            flux_ref[face, 8 * k : 8 * k + 8, :] = flux[k]

    row = iota((8, LANES), 0)
    lane = iota((8, LANES), 1)
    even = 2 * (row % 4)

    def restrict(comp, _, box):
        at = pl.ds(pl.multiple_of(comp * 8, 8), 8)
        faces = [
            flux_ref[box * 6 + side, at, :] * (0.125 if side % 2 == 0 else -0.125)
            for side in range(6)
        ]
        for side in range(6):
            face = faces[side]
            if side < 2:
                face = face + roll(face, -1, 1)
                face = face + roll(face, -EDGE, 1)
                face = lane_gather(face, 64 * ((lane // HALF) % 2) + 2 * (lane % HALF))
            else:
                face = face + roll(face, -1, 0)
                face = face + roll(face, -1 if side < 4 else -EDGE, 1)
                face = row_gather(face, even)
            faces[side] = face
        for t in range(2):
            quarter = 2 * t + row // 4
            for h in range(2):
                spot = (box, comp, slice(8 * t, 8 * t + 8), slice(LANES * h, LANES * h + LANES))
                cells = interior_ref[spot]
                pick = 64 * ((lane // HALF) % 2) + 8 * quarter + 4 * h + lane // 32
                cells = cells + jnp.where(lane % HALF == 0, lane_gather(faces[4], pick), 0.0)
                cells = cells + jnp.where(
                    lane % HALF == HALF - 1, lane_gather(faces[5], pick), 0.0
                )
                pick = 32 * quarter + 2 * (lane % HALF)
                near_edge = lane < HALF if h == 0 else lane >= LANES - HALF
                cells = cells + jnp.where(near_edge, lane_gather(faces[2 + h], pick), 0.0)
                first = row == 0 if t == 0 else row == 7
                cells = cells + jnp.where(first, row_gather(faces[t], 4 * h + lane // 32), 0.0)
                coarse_ref[spot] = cells
        return 0

    def each(box, act):
        for i in range(send_ref.shape[0]):

            @pl.when(wanted[i, me] == box + 1)
            def _(i=i):
                act(pltpu.make_async_copy(coarse_ref.at[box], send_ref.at[i], sems.at[i]))

    for fetch in fetches:
        fetch.wait()
    for box in range(boxes):
        lax.fori_loop(0, COMPS, functools.partial(restrict, box=box), 0)
        each(box, lambda copy: copy.start())
    for box in range(boxes):
        each(box, lambda copy: copy.wait())


def finish_kernel(boxes, partial_ref, flux_ref, out_ref):
    row = iota((8, LANES), 0)
    lane = iota((8, LANES), 1)
    inner = lane % 32

    def plane(step, _):
        box = step // COMPS
        comp = step % COMPS
        at = pl.ds(pl.multiple_of(comp * 8, 8), 8)
        faces = [flux_ref[box * 6 + side, at, :] for side in range(6)]
        for q in range(4):
            for v in range(8):
                spot = (box, comp, slice(8 * q, 8 * q + 8), slice(LANES * v, LANES * v + LANES))
                cells = partial_ref[spot]
                shift = 8 * q + v
                cells = cells + jnp.where(inner == 0, roll(faces[4], -shift, 1), 0.0)
                cells = cells - jnp.where(inner == 31, roll(faces[5], 31 - shift, 1), 0.0)
                if v == 0:
                    cells = cells + jnp.where(lane < 32, roll(faces[2], -32 * q, 1), 0.0)
                if v == 7:
                    cells = cells - jnp.where(lane >= 96, roll(faces[3], 96 - 32 * q, 1), 0.0)
                if q == 0:
                    cells = cells + jnp.where(row == 0, faces[0][v : v + 1], 0.0)
                if q == 3:
                    cells = cells - jnp.where(row == 7, faces[1][v : v + 1], 0.0)
                out_ref[spot] = cells
        return 0

    lax.fori_loop(0, boxes * COMPS, plane, 0)


def copy_kernel(x_ref, out_ref):
    out_ref[...] = x_ref[...]


def place_kernel(boxes, line_size, covering_ref, _, source_ref, out_ref, sems):
    def each(act):
        for i in range(out_ref.shape[0]):
            box = covering_ref[i]

            @pl.when(box >= 0)
            def _(i=i, box=box):
                column = quotient(quotient(box, boxes), line_size)
                column = jnp.clip(column, 0, source_ref.shape[0] - 1)
                act(pltpu.make_async_copy(source_ref.at[column], out_ref.at[i], sems.at[i]))

    each(lambda copy: copy.start())
    each(lambda copy: copy.wait())


def any_spec():
    return pl.BlockSpec(memory_space=pl.ANY)


def hbm_spec():
    return pl.BlockSpec(memory_space=pltpu.HBM)


def smem_spec():
    return pl.BlockSpec(memory_space=pltpu.SMEM)


def vmem_spec():
    return pl.BlockSpec(memory_space=pltpu.VMEM)


def kernel_params(mib=16):
    return pltpu.CompilerParams(vmem_limit_bytes=mib << 20)


def near(x):
    return pltpu.with_memory_space_constraint(x, pltpu.VMEM)


def far(x):
    return pltpu.with_memory_space_constraint(x, pltpu.HBM)


def exchange(x):
    return lax.all_to_all(x, PLANE, split_axis=0, concat_axis=0, tiled=True)


def body(fine_state, coarse_state, neighbours, coarse_sources, covering):
    boxes = fine_state.shape[0]
    blocks = coarse_state.shape[0]
    line_size = lax.axis_size("gy") * lax.axis_size("gz")
    ring = lax.axis_size("gx")
    f32 = jnp.float32

    tile = (ring, LANES)

    def across(x, bit):
        return lax.ppermute(x, "gx", [(i, i ^ bit) for i in range(ring)])

    requests, wants = pl.pallas_call(
        functools.partial(request_kernel, boxes, blocks, line_size),
        out_shape=(
            jax.ShapeDtypeStruct((line_size, LANES), jnp.int32),
            pltpu.VMEM(tile, jnp.int32),
        ),
        in_specs=[smem_spec()] * 3,
        out_specs=(vmem_spec(), vmem_spec()),
        name="requests",
    )(far(neighbours), far(coarse_sources), far(covering))
    other = across(wants, 4)
    codes = exchange(requests)

    table = pl.pallas_call(
        functools.partial(table_kernel, boxes, blocks),
        out_shape=pltpu.VMEM((6 * (boxes + blocks), SLOT_ROWS, LANES), f32),
        in_specs=[vmem_spec(), vmem_spec()],
        out_specs=vmem_spec(),
        name="tables",
    )(fine_state, coarse_state)

    answers, wants = pl.pallas_call(
        reply_kernel,
        out_shape=(
            pltpu.HBM((line_size, SLOT_ROWS, LANES), f32),
            pltpu.VMEM(tile, jnp.int32),
        ),
        in_specs=[vmem_spec()] * 4,
        out_specs=(hbm_spec(), vmem_spec()),
        scratch_shapes=[
            pltpu.SMEM((line_size, LANES), jnp.int32),
            pltpu.SemaphoreType.DMA,
            pltpu.SemaphoreType.DMA((line_size,)),
        ],
        compiler_params=kernel_params(),
        name="answers",
    )(near(codes), near(table), near(wants), near(other))
    other = across(wants, 1)
    replies = exchange(answers)

    partial, interior, wants = pl.pallas_call(
        functools.partial(interior_kernel, boxes),
        out_shape=(
            pltpu.HBM(fine_state.shape, f32),
            pltpu.HBM((boxes, COMPS, HALF, SMALL), f32),
            pltpu.VMEM(tile, jnp.int32),
        ),
        in_specs=[vmem_spec()] * 3,
        out_specs=(hbm_spec(), hbm_spec(), vmem_spec()),
        scratch_shapes=[
            pltpu.VMEM(fine_state.shape, f32),
            pltpu.VMEM((boxes, COMPS, HALF, SMALL), f32),
        ]
        + [pltpu.VMEM((EDGE, boxes * FLAT), f32)] * 3
        + [pltpu.VMEM((8, EDGE, LANES), f32), pltpu.SemaphoreType.DMA((2,))],
        compiler_params=kernel_params(),
        name="interior",
    )(fine_state, near(wants), near(other))
    other = across(wants, 2)


    flux, sent = pl.pallas_call(
        functools.partial(flux_kernel, boxes, blocks, line_size),
        out_shape=(
            pltpu.VMEM((6 * boxes, SLOT_ROWS, LANES), f32),
            pltpu.HBM((ring, COMPS, HALF, SMALL), f32),
        ),
        in_specs=[smem_spec()] * 2 + [hbm_spec()] + [vmem_spec()] * 4,
        out_specs=(vmem_spec(), hbm_spec()),
        scratch_shapes=[
            pltpu.VMEM((boxes, COMPS, HALF, SMALL), f32),
            pltpu.VMEM((boxes, COMPS, HALF, SMALL), f32),
            pltpu.VMEM(tile, jnp.int32),
            pltpu.SMEM(tile, jnp.int32),
            pltpu.SemaphoreType.DMA((2,)),
            pltpu.SemaphoreType.DMA((ring,)),
        ],
        compiler_params=kernel_params(),
        name="fluxes",
    )(
        far(neighbours),
        far(coarse_sources),
        far(interior),
        near(table),
        near(replies),
        near(wants),
        near(other),
    )
    received = lax.all_to_all(sent, "gx", split_axis=0, concat_axis=0, tiled=True)

    fine_next = pl.pallas_call(
        functools.partial(finish_kernel, boxes),
        out_shape=jax.ShapeDtypeStruct(fine_state.shape, f32),
        in_specs=[vmem_spec(), vmem_spec()],
        out_specs=vmem_spec(),
        compiler_params=kernel_params(),
        name="finish",
    )(partial, near(flux))

    prior = pl.pallas_call(
        copy_kernel,
        out_shape=jax.ShapeDtypeStruct(coarse_state.shape, f32),
        in_specs=[vmem_spec()],
        out_specs=vmem_spec(),
        compiler_params=kernel_params(),
        name="prior",
    )(coarse_state)

    coarse_next = pl.pallas_call(
        functools.partial(place_kernel, boxes, line_size),
        out_shape=jax.ShapeDtypeStruct(coarse_state.shape, f32),
        in_specs=[smem_spec(), any_spec(), vmem_spec()],
        out_specs=any_spec(),
        scratch_shapes=[pltpu.SemaphoreType.DMA((blocks,))],
        input_output_aliases={1: 0},
        compiler_params=kernel_params(),
        name="place",
    )(far(covering), prior, near(received))
    return fine_next, coarse_next


def solution(mesh):
    spec = P(AXES)
    return jax.shard_map(
        body, mesh=mesh, in_specs=(spec,) * 5, out_specs=(spec, spec), check_vma=False
    )
```

```python
import functools

import jax
import jax.numpy as jnp
from jax import lax
from jax.experimental import pallas as pl
from jax.experimental.pallas import tpu as pltpu
from jax.sharding import PartitionSpec as P


adiabatic = 5.0 / 3.0
courant = 0.12
AXES = ("gx", "gy", "gz")
PLANE = ("gy", "gz")

EDGE = 32
HALF = 16
FLAT = EDGE * EDGE
SMALL = HALF * HALF
LANES = 128
COMPS = 5
SLOT_ROWS = COMPS * FLAT // LANES


def iota(shape, dim):
    return lax.broadcasted_iota(jnp.int32, shape, dim)


def roll(x, shift, axis):
    size = x.shape[axis]
    shift = shift % size
    return x if shift == 0 else pltpu.roll(x, shift, axis)


def quotient(x, n):
    return lax.shift_right_logical(x, n.bit_length() - 1) if n & (n - 1) == 0 else lax.div(x, n)


def remainder(x, n):
    return lax.bitwise_and(x, n - 1) if n & (n - 1) == 0 else lax.rem(x, n)


def face_source(fine_ref, coarse_ref, box, side, boxes, blocks, line_size):
    fine_id = fine_ref[box, side]
    coarse_id = coarse_ref[box, side]
    is_fine = fine_id >= 0
    device = jnp.where(is_fine, quotient(fine_id, boxes), quotient(coarse_id, blocks))
    row = jnp.where(
        is_fine,
        remainder(fine_id, boxes) * 6 + (side ^ 1),
        boxes * 6 + remainder(coarse_id, blocks) * 6 + (side ^ 1),
    )
    return remainder(device, line_size), row


def request_kernel(
    boxes, blocks, line_size, fine_ref, coarse_ref, covering_ref, out_ref, wants_ref
):
    peers = iota(out_ref.shape, 0)
    table = jnp.zeros(out_ref.shape, jnp.int32)
    for box in range(boxes):
        for side in range(6):
            peer, row = face_source(fine_ref, coarse_ref, box, side, boxes, blocks, line_size)
            table = jnp.where(peers == peer, row + 1, table)
    out_ref[...] = table
    column = jnp.where(
        iota(wants_ref.shape, 0) == lax.axis_index("gx"), iota(wants_ref.shape, 1), -1
    )
    wants = jnp.zeros(wants_ref.shape, jnp.int32)
    for i in range(blocks):
        box = covering_ref[i]
        owner = jnp.where(box >= 0, quotient(quotient(box, boxes), line_size), -2)
        wants = jnp.where(column == owner, remainder(box, boxes) + 1, wants)
    wants_ref[...] = wants


def lane_gather(x, index):
    return jnp.take_along_axis(x, index, axis=1)


def row_gather(x, index):
    return jnp.take_along_axis(x, index, axis=0)


def table_kernel(boxes, blocks, fine_ref, coarse_ref, out_ref):
    row = iota((8, LANES), 0)
    lane = iota((8, LANES), 1)
    quad = lane // 32
    inner = lane % 32

    def fine_box(box, _):
        base = box * 6
        for comp in range(COMPS):
            dst = slice(8 * comp, 8 * comp + 8)
            for side, first in ((0, 0), (1, EDGE - 1)):
                for r in range(8):
                    out_ref[base + side, 8 * comp + r : 8 * comp + r + 1, :] = fine_ref[
                        box, comp, first : first + 1, LANES * r : LANES * r + LANES
                    ]
            y_low = jnp.zeros((8, LANES), jnp.float32)
            y_high = y_low
            z_low = y_low
            z_high = y_low
            for q in range(4):
                for v in range(8):
                    cells = fine_ref[box, comp, 8 * q : 8 * q + 8, LANES * v : LANES * v + LANES]
                    if v == 0:
                        y_low = jnp.where(quad == q, roll(cells, 32 * q, 1), y_low)
                    if v == 7:
                        y_high = jnp.where(quad == q, roll(cells, 32 * q - 96, 1), y_high)
                    spot = inner == 8 * q + v
                    z_low = jnp.where(spot, roll(cells, 8 * q + v, 1), z_low)
                    z_high = jnp.where(spot, roll(cells, 8 * q + v - 31, 1), z_high)
            out_ref[base + 2, dst, :] = y_low
            out_ref[base + 3, dst, :] = y_high
            out_ref[base + 4, dst, :] = z_low
            out_ref[base + 5, dst, :] = z_high
        return 0

    lax.fori_loop(0, boxes, fine_box, 0)

    pick_x = 32 * (row % 4) + 16 * (quad // 2) + inner // 2
    pick_y = inner // 2
    pick_z = 32 * (inner % 4) + 16 * (quad // 2)
    rows_y = 4 * (quad % 2) + row // 2
    rows_z = 4 * ((inner // 8) % 2) + row // 2

    def coarse_block(block, _):
        base = boxes * 6 + block * 6
        for comp in range(COMPS):
            dst = slice(8 * comp, 8 * comp + 8)
            cells = [
                [
                    coarse_ref[block, comp, 8 * g : 8 * g + 8, LANES * h : LANES * h + LANES]
                    for h in range(2)
                ]
                for g in range(2)
            ]
            for side, first in ((0, 0), (1, HALF - 1)):
                parts = [
                    jnp.broadcast_to(cells[first // 8][h][first % 8 : first % 8 + 1], (8, LANES))
                    for h in range(2)
                ]
                out_ref[base + side, dst, :] = jnp.where(
                    row < 4, lane_gather(parts[0], pick_x), lane_gather(parts[1], pick_x)
                )
            for side, half, start in ((2, 0, 0), (3, 1, LANES - HALF)):
                parts = [
                    row_gather(lane_gather(cells[g][half], pick_y + start), rows_y)
                    for g in range(2)
                ]
                out_ref[base + side, dst, :] = jnp.where(quad < 2, parts[0], parts[1])
            for side, last in ((4, 0), (5, HALF - 1)):
                parts = [
                    row_gather(
                        jnp.where(
                            inner % 8 < 4,
                            lane_gather(cells[g][0], pick_z + last),
                            lane_gather(cells[g][1], pick_z + last),
                        ),
                        rows_z,
                    )
                    for g in range(2)
                ]
                out_ref[base + side, dst, :] = jnp.where(inner < 16, parts[0], parts[1])
        return 0

    lax.fori_loop(0, blocks, coarse_block, 0, unroll=2)


def primitives(cells):
    inverse = 1.0 / cells[0]
    kinetic = (
        0.5 * (cells[1] * cells[1] + cells[2] * cells[2] + cells[3] * cells[3]) * inverse
    )
    pressure = (adiabatic - 1.0) * (cells[4] - kinetic)
    sound = jnp.sqrt(adiabatic * pressure * inverse)
    return inverse, pressure, sound


def physical_flux(cells, normal, speed, pressure):
    entries = [
        cells[normal],
        cells[1] * speed,
        cells[2] * speed,
        cells[3] * speed,
        (cells[4] + pressure) * speed,
    ]
    entries[normal] = entries[normal] + pressure
    return entries


def face_flux(low, high, low_flux, high_flux, low_fast, high_fast):
    fastest = jnp.maximum(low_fast, high_fast)
    return [
        (low_flux[k] + high_flux[k]) - fastest * (high[k] - low[k]) for k in range(COMPS)
    ]


def add_steps(total, cells, normal, speed, pressure, fast, keep, step, axis):
    flux = physical_flux(cells, normal, speed, pressure)
    upper = face_flux(
        cells,
        [roll(c, -step, axis) for c in cells],
        flux,
        [roll(c, -step, axis) for c in flux],
        fast,
        roll(fast, -step, axis),
    )
    upper = [jnp.where(keep, c, 0.0) for c in upper]
    steps = [c - roll(c, step, axis) for c in upper]
    return steps if total is None else [total[k] + steps[k] for k in range(COMPS)]


def interior_kernel(
    boxes,
    fine_ref,
    wants_a,
    wants_b,
    partial_ref,
    restricted_ref,
    wants_ref,
    out_ref,
    coarse_ref,
    speed_ref,
    pressure_ref,
    fast_ref,
    pair_ref,
    sems,
):
    wants_ref[...] = wants_a[...] + wants_b[...]
    columns = FLAT // LANES
    row = iota((EDGE, LANES), 0)
    lane = iota((EDGE, LANES), 1)

    def column(step, _):
        box = step // columns
        at = pl.ds(pl.multiple_of((step % columns) * LANES, LANES), LANES)
        cells = [fine_ref[box, k, :, at] for k in range(COMPS)]
        inverse, pressure, sound = primitives(cells)
        speed_y = cells[2] * inverse
        there = pl.ds(pl.multiple_of(step * LANES, LANES), LANES)
        speed_ref[:, there] = speed_y
        pressure_ref[:, there] = pressure
        fast_ref[:, there] = jnp.abs(speed_y) + sound
        total = None
        for normal, axis, keep in ((1, 0, row < EDGE - 1), (3, 1, lane % EDGE < EDGE - 1)):
            speed = cells[normal] * inverse
            total = add_steps(
                total, cells, normal, speed, pressure, jnp.abs(speed) + sound, keep, 1, axis
            )
        for k in range(COMPS):
            out_ref[box, k, :, at] = total[k]
        return 0

    lax.fori_loop(0, boxes * columns, column, 0, unroll=2)
    wide = iota((8, FLAT), 1)

    def rows(step, _):
        box = step // 4
        at = pl.ds(pl.multiple_of((step % 4) * 8, 8), 8)
        along = pl.ds(pl.multiple_of(box * FLAT, FLAT), FLAT)
        cells = [fine_ref[box, k, at, :] for k in range(COMPS)]
        speed, pressure, fast = [ref[at, along] for ref in (speed_ref, pressure_ref, fast_ref)]
        total = [out_ref[box, k, at, :] for k in range(COMPS)]
        keep = wide < FLAT - EDGE
        total = add_steps(total, cells, 2, speed, pressure, fast, keep, EDGE, 1)
        for k in range(COMPS):
            out_ref[box, k, at, :] = cells[k] - (0.5 * courant) * total[k]
        return 0

    lax.fori_loop(0, boxes * 4, rows, 0)
    save = pltpu.make_async_copy(out_ref, partial_ref, sems.at[0])
    save.start()
    lane16 = iota((HALF, LANES), 1)
    pick = 64 * ((lane16 // HALF) % 2) + 2 * (lane16 % HALF)

    def restrict(step, _):
        box = step // COMPS
        comp = step % COMPS
        for h in range(2):
            total = jnp.zeros((HALF, LANES), jnp.float32)
            for w in range(4):
                v = 4 * h + w
                pair_ref[v] = out_ref[box, comp, :, LANES * v : LANES * v + LANES]
                pair = (
                    pair_ref[v, pl.ds(0, HALF, stride=2), :]
                    + pair_ref[v, pl.ds(1, HALF, stride=2), :]
                )
                pair = pair + roll(pair, -EDGE, 1)
                pair = pair + roll(pair, -1, 1)
                total = jnp.where(lane16 // 32 == w, lane_gather(pair, pick), total)
            coarse_ref[box, comp, :, LANES * h : LANES * h + LANES] = 0.125 * total
        return 0

    lax.fori_loop(0, boxes * COMPS, restrict, 0, unroll=2)
    last = pltpu.make_async_copy(coarse_ref, restricted_ref, sems.at[1])
    last.start()
    save.wait()
    last.wait()


def reply_kernel(code_ref, table_ref, wants_a, wants_b, out_ref, wants_ref, codes, sem, sems):
    slots = out_ref.shape[0]
    rows = table_ref.shape[0]
    copy = pltpu.make_async_copy(code_ref, codes, sem)
    copy.start()
    copy.wait()

    def each(act):
        for i in range(slots):
            code = codes[i, 0]

            @pl.when(code > 0)
            def _(i=i, code=code):
                source = table_ref.at[jnp.clip(code - 1, 0, rows - 1)]
                act(pltpu.make_async_copy(source, out_ref.at[i], sems.at[i]))

    each(lambda copy: copy.start())
    wants_ref[...] = wants_a[...] + wants_b[...]
    each(lambda copy: copy.wait())


def flux_kernel(
    boxes,
    blocks,
    line_size,
    fine_ids,
    coarse_ids,
    restricted_ref,
    table_ref,
    replies_ref,
    wants_a,
    wants_b,
    flux_ref,
    send_ref,
    interior_ref,
    coarse_ref,
    wants_ref,
    wanted,
    fetch_sems,
    sems,
):
    me = lax.axis_index("gx")
    wants_ref[...] = wants_a[...] + wants_b[...]
    fetches = [
        pltpu.make_async_copy(wants_ref, wanted, fetch_sems.at[0]),
        pltpu.make_async_copy(restricted_ref, interior_ref, fetch_sems.at[1]),
    ]
    for fetch in fetches:
        fetch.start()
    for face in range(6 * boxes):
        box, side = face // 6, face % 6
        normal = side // 2 + 1
        peer, _ = face_source(fine_ids, coarse_ids, box, side, boxes, blocks, line_size)
        own = [table_ref[face, 8 * k : 8 * k + 8, :] for k in range(COMPS)]
        ghost = [replies_ref[peer, 8 * k : 8 * k + 8, :] for k in range(COMPS)]
        sides = []
        for cells in (own, ghost):
            inverse, pressure, sound = primitives(cells)
            speed = cells[normal] * inverse
            flux = physical_flux(cells, normal, speed, pressure)
            sides.append((cells, flux, jnp.abs(speed) + sound))
        low, high = sides[::-1] if side % 2 == 0 else sides
        flux = face_flux(low[0], high[0], low[1], high[1], low[2], high[2])
        flux = [(0.5 * courant) * c for c in flux]
        for k in range(COMPS):
            flux_ref[face, 8 * k : 8 * k + 8, :] = flux[k]

    row = iota((8, LANES), 0)
    lane = iota((8, LANES), 1)
    even = 2 * (row % 4)

    def restrict(comp, box):
        at = slice(8 * comp, 8 * comp + 8)
        faces = [
            flux_ref[box * 6 + side, at, :] * (0.125 if side % 2 == 0 else -0.125)
            for side in range(6)
        ]
        for side in range(6):
            face = faces[side]
            if side < 2:
                face = face + roll(face, -1, 1)
                face = face + roll(face, -EDGE, 1)
                face = lane_gather(face, 64 * ((lane // HALF) % 2) + 2 * (lane % HALF))
            else:
                face = face + roll(face, -1, 0)
                face = face + roll(face, -1 if side < 4 else -EDGE, 1)
                face = row_gather(face, even)
            faces[side] = face
        for t in range(2):
            quarter = 2 * t + row // 4
            for h in range(2):
                spot = (box, comp, slice(8 * t, 8 * t + 8), slice(LANES * h, LANES * h + LANES))
                cells = interior_ref[spot]
                pick = 64 * ((lane // HALF) % 2) + 8 * quarter + 4 * h + lane // 32
                cells = cells + jnp.where(lane % HALF == 0, lane_gather(faces[4], pick), 0.0)
                cells = cells + jnp.where(
                    lane % HALF == HALF - 1, lane_gather(faces[5], pick), 0.0
                )
                pick = 32 * quarter + 2 * (lane % HALF)
                near_edge = lane < HALF if h == 0 else lane >= LANES - HALF
                cells = cells + jnp.where(near_edge, lane_gather(faces[2 + h], pick), 0.0)
                first = row == 0 if t == 0 else row == 7
                cells = cells + jnp.where(first, row_gather(faces[t], 4 * h + lane // 32), 0.0)
                coarse_ref[spot] = cells

    def each(box, act):
        for i in range(send_ref.shape[0]):

            @pl.when(wanted[i, me] == box + 1)
            def _(i=i):
                act(pltpu.make_async_copy(coarse_ref.at[box], send_ref.at[i], sems.at[i]))

    for fetch in fetches:
        fetch.wait()
    for box in range(boxes):
        for comp in range(COMPS):
            restrict(comp, box)
        each(box, lambda copy: copy.start())
    for box in range(boxes):
        each(box, lambda copy: copy.wait())


def finish_kernel(boxes, partial_ref, flux_ref, out_ref):
    row = iota((8, LANES), 0)
    lane = iota((8, LANES), 1)
    inner = lane % 32

    def plane(step, _):
        box = step // COMPS
        comp = step % COMPS
        at = pl.ds(pl.multiple_of(comp * 8, 8), 8)
        faces = [flux_ref[box * 6 + side, at, :] for side in range(6)]
        for q in range(4):
            for v in range(8):
                spot = (box, comp, slice(8 * q, 8 * q + 8), slice(LANES * v, LANES * v + LANES))
                cells = partial_ref[spot]
                shift = 8 * q + v
                cells = cells + jnp.where(inner == 0, roll(faces[4], -shift, 1), 0.0)
                cells = cells - jnp.where(inner == 31, roll(faces[5], 31 - shift, 1), 0.0)
                if v == 0:
                    cells = cells + jnp.where(lane < 32, roll(faces[2], -32 * q, 1), 0.0)
                if v == 7:
                    cells = cells - jnp.where(lane >= 96, roll(faces[3], 96 - 32 * q, 1), 0.0)
                if q == 0:
                    cells = cells + jnp.where(row == 0, faces[0][v : v + 1], 0.0)
                if q == 3:
                    cells = cells - jnp.where(row == 7, faces[1][v : v + 1], 0.0)
                out_ref[spot] = cells
        return 0

    lax.fori_loop(0, boxes * COMPS, plane, 0)


def copy_kernel(x_ref, out_ref):
    out_ref[...] = x_ref[...]


def place_kernel(boxes, line_size, covering_ref, _, source_ref, out_ref, sems):
    def each(act):
        for i in range(out_ref.shape[0]):
            box = covering_ref[i]

            @pl.when(box >= 0)
            def _(i=i, box=box):
                column = quotient(quotient(box, boxes), line_size)
                column = jnp.clip(column, 0, source_ref.shape[0] - 1)
                act(pltpu.make_async_copy(source_ref.at[column], out_ref.at[i], sems.at[i]))

    each(lambda copy: copy.start())
    each(lambda copy: copy.wait())


def any_spec():
    return pl.BlockSpec(memory_space=pl.ANY)


def hbm_spec():
    return pl.BlockSpec(memory_space=pltpu.HBM)


def smem_spec():
    return pl.BlockSpec(memory_space=pltpu.SMEM)


def vmem_spec():
    return pl.BlockSpec(memory_space=pltpu.VMEM)


def kernel_params(mib=16):
    return pltpu.CompilerParams(vmem_limit_bytes=mib << 20)


def near(x):
    return pltpu.with_memory_space_constraint(x, pltpu.VMEM)


def far(x):
    return pltpu.with_memory_space_constraint(x, pltpu.HBM)


def exchange(x):
    return lax.all_to_all(x, PLANE, split_axis=0, concat_axis=0, tiled=True)


def body(fine_state, coarse_state, neighbours, coarse_sources, covering):
    boxes = fine_state.shape[0]
    blocks = coarse_state.shape[0]
    line_size = lax.axis_size("gy") * lax.axis_size("gz")
    ring = lax.axis_size("gx")
    f32 = jnp.float32

    tile = (ring, LANES)

    def across(x, bit):
        return lax.ppermute(x, "gx", [(i, i ^ bit) for i in range(ring)])

    requests, wants = pl.pallas_call(
        functools.partial(request_kernel, boxes, blocks, line_size),
        out_shape=(
            jax.ShapeDtypeStruct((line_size, LANES), jnp.int32),
            pltpu.VMEM(tile, jnp.int32),
        ),
        in_specs=[smem_spec()] * 3,
        out_specs=(vmem_spec(), vmem_spec()),
        name="requests",
    )(far(neighbours), far(coarse_sources), far(covering))
    other = across(wants, 4)
    codes = exchange(requests)

    table = pl.pallas_call(
        functools.partial(table_kernel, boxes, blocks),
        out_shape=pltpu.VMEM((6 * (boxes + blocks), SLOT_ROWS, LANES), f32),
        in_specs=[vmem_spec(), vmem_spec()],
        out_specs=vmem_spec(),
        name="tables",
    )(fine_state, coarse_state)

    answers, wants = pl.pallas_call(
        reply_kernel,
        out_shape=(
            pltpu.HBM((line_size, SLOT_ROWS, LANES), f32),
            pltpu.VMEM(tile, jnp.int32),
        ),
        in_specs=[vmem_spec()] * 4,
        out_specs=(hbm_spec(), vmem_spec()),
        scratch_shapes=[
            pltpu.SMEM((line_size, LANES), jnp.int32),
            pltpu.SemaphoreType.DMA,
            pltpu.SemaphoreType.DMA((line_size,)),
        ],
        compiler_params=kernel_params(),
        name="answers",
    )(near(codes), near(table), near(wants), near(other))
    other = across(wants, 1)
    replies = exchange(answers)

    partial, interior, wants = pl.pallas_call(
        functools.partial(interior_kernel, boxes),
        out_shape=(
            pltpu.HBM(fine_state.shape, f32),
            pltpu.HBM((boxes, COMPS, HALF, SMALL), f32),
            pltpu.VMEM(tile, jnp.int32),
        ),
        in_specs=[vmem_spec()] * 3,
        out_specs=(hbm_spec(), hbm_spec(), vmem_spec()),
        scratch_shapes=[
            pltpu.VMEM(fine_state.shape, f32),
            pltpu.VMEM((boxes, COMPS, HALF, SMALL), f32),
        ]
        + [pltpu.VMEM((EDGE, boxes * FLAT), f32)] * 3
        + [pltpu.VMEM((8, EDGE, LANES), f32), pltpu.SemaphoreType.DMA((2,))],
        compiler_params=kernel_params(),
        name="interior",
    )(fine_state, near(wants), near(other))
    other = across(wants, 2)


    flux, sent = pl.pallas_call(
        functools.partial(flux_kernel, boxes, blocks, line_size),
        out_shape=(
            pltpu.VMEM((6 * boxes, SLOT_ROWS, LANES), f32),
            pltpu.HBM((ring, COMPS, HALF, SMALL), f32),
        ),
        in_specs=[smem_spec()] * 2 + [hbm_spec()] + [vmem_spec()] * 4,
        out_specs=(vmem_spec(), hbm_spec()),
        scratch_shapes=[
            pltpu.VMEM((boxes, COMPS, HALF, SMALL), f32),
            pltpu.VMEM((boxes, COMPS, HALF, SMALL), f32),
            pltpu.VMEM(tile, jnp.int32),
            pltpu.SMEM(tile, jnp.int32),
            pltpu.SemaphoreType.DMA((2,)),
            pltpu.SemaphoreType.DMA((ring,)),
        ],
        compiler_params=kernel_params(),
        name="fluxes",
    )(
        far(neighbours),
        far(coarse_sources),
        far(interior),
        near(table),
        near(replies),
        near(wants),
        near(other),
    )
    received = lax.all_to_all(sent, "gx", split_axis=0, concat_axis=0, tiled=True)

    fine_next = pl.pallas_call(
        functools.partial(finish_kernel, boxes),
        out_shape=jax.ShapeDtypeStruct(fine_state.shape, f32),
        in_specs=[vmem_spec(), vmem_spec()],
        out_specs=vmem_spec(),
        compiler_params=kernel_params(),
        name="finish",
    )(partial, near(flux))

    prior = pl.pallas_call(
        copy_kernel,
        out_shape=jax.ShapeDtypeStruct(coarse_state.shape, f32),
        in_specs=[vmem_spec()],
        out_specs=vmem_spec(),
        compiler_params=kernel_params(),
        name="prior",
    )(coarse_state)

    coarse_next = pl.pallas_call(
        functools.partial(place_kernel, boxes, line_size),
        out_shape=jax.ShapeDtypeStruct(coarse_state.shape, f32),
        in_specs=[smem_spec(), any_spec(), vmem_spec()],
        out_specs=any_spec(),
        scratch_shapes=[pltpu.SemaphoreType.DMA((blocks,))],
        input_output_aliases={1: 0},
        compiler_params=kernel_params(),
        name="place",
    )(far(covering), prior, near(received))
    return fine_next, coarse_next


def solution(mesh):
    spec = P(AXES)
    return jax.shard_map(
        body, mesh=mesh, in_specs=(spec,) * 5, out_specs=(spec, spec), check_vma=False
    )
```

```python
import functools

import jax
import jax.numpy as jnp
from jax import lax
from jax.experimental import pallas as pl
from jax.experimental.pallas import tpu as pltpu
from jax.sharding import PartitionSpec as P


adiabatic = 5.0 / 3.0
courant = 0.12
AXES = ("gx", "gy", "gz")
PLANE = ("gy", "gz")

EDGE = 32
HALF = 16
FLAT = EDGE * EDGE
SMALL = HALF * HALF
LANES = 128
COMPS = 5
SLOT_ROWS = COMPS * FLAT // LANES


def iota(shape, dim):
    return lax.broadcasted_iota(jnp.int32, shape, dim)


def roll(x, shift, axis):
    size = x.shape[axis]
    shift = shift % size
    return x if shift == 0 else pltpu.roll(x, shift, axis)


def quotient(x, n):
    return lax.shift_right_logical(x, n.bit_length() - 1) if n & (n - 1) == 0 else lax.div(x, n)


def remainder(x, n):
    return lax.bitwise_and(x, n - 1) if n & (n - 1) == 0 else lax.rem(x, n)


def face_source(fine_ref, coarse_ref, box, side, boxes, blocks, line_size):
    fine_id = fine_ref[box, side]
    coarse_id = coarse_ref[box, side]
    is_fine = fine_id >= 0
    device = jnp.where(is_fine, quotient(fine_id, boxes), quotient(coarse_id, blocks))
    row = jnp.where(
        is_fine,
        remainder(fine_id, boxes) * 6 + (side ^ 1),
        boxes * 6 + remainder(coarse_id, blocks) * 6 + (side ^ 1),
    )
    return remainder(device, line_size), row


def request_kernel(boxes, blocks, line_size, fine_ref, coarse_ref, out_ref):
    peers = iota(out_ref.shape, 0)
    table = jnp.zeros(out_ref.shape, jnp.int32)
    for box in range(boxes):
        for side in range(6):
            peer, row = face_source(fine_ref, coarse_ref, box, side, boxes, blocks, line_size)
            table = jnp.where(peers == peer, row + 1, table)
    out_ref[...] = table


def lane_gather(x, index):
    return jnp.take_along_axis(x, index, axis=1)


def row_gather(x, index):
    return jnp.take_along_axis(x, index, axis=0)


def table_kernel(boxes, blocks, fine_ref, coarse_ref, out_ref):
    row = iota((8, LANES), 0)
    lane = iota((8, LANES), 1)
    quad = lane // 32
    inner = lane % 32

    def fine_box(box, _):
        base = box * 6
        for comp in range(COMPS):
            dst = slice(8 * comp, 8 * comp + 8)
            for side, first in ((0, 0), (1, EDGE - 1)):
                for r in range(8):
                    out_ref[base + side, 8 * comp + r : 8 * comp + r + 1, :] = fine_ref[
                        box, comp, first : first + 1, LANES * r : LANES * r + LANES
                    ]
            y_low = jnp.zeros((8, LANES), jnp.float32)
            y_high = y_low
            z_low = y_low
            z_high = y_low
            for q in range(4):
                for v in range(8):
                    cells = fine_ref[box, comp, 8 * q : 8 * q + 8, LANES * v : LANES * v + LANES]
                    if v == 0:
                        y_low = jnp.where(quad == q, roll(cells, 32 * q, 1), y_low)
                    if v == 7:
                        y_high = jnp.where(quad == q, roll(cells, 32 * q - 96, 1), y_high)
                    spot = inner == 8 * q + v
                    z_low = jnp.where(spot, roll(cells, 8 * q + v, 1), z_low)
                    z_high = jnp.where(spot, roll(cells, 8 * q + v - 31, 1), z_high)
            out_ref[base + 2, dst, :] = y_low
            out_ref[base + 3, dst, :] = y_high
            out_ref[base + 4, dst, :] = z_low
            out_ref[base + 5, dst, :] = z_high
        return 0

    lax.fori_loop(0, boxes, fine_box, 0)

    pick_x = 32 * (row % 4) + 16 * (quad // 2) + inner // 2
    pick_y = inner // 2
    pick_z = 32 * (inner % 4) + 16 * (quad // 2)
    rows_y = 4 * (quad % 2) + row // 2
    rows_z = 4 * ((inner // 8) % 2) + row // 2

    def coarse_block(block, _):
        base = boxes * 6 + block * 6
        for comp in range(COMPS):
            dst = slice(8 * comp, 8 * comp + 8)
            cells = [
                [
                    coarse_ref[block, comp, 8 * g : 8 * g + 8, LANES * h : LANES * h + LANES]
                    for h in range(2)
                ]
                for g in range(2)
            ]
            for side, first in ((0, 0), (1, HALF - 1)):
                parts = [
                    jnp.broadcast_to(cells[first // 8][h][first % 8 : first % 8 + 1], (8, LANES))
                    for h in range(2)
                ]
                out_ref[base + side, dst, :] = jnp.where(
                    row < 4, lane_gather(parts[0], pick_x), lane_gather(parts[1], pick_x)
                )
            for side, half, start in ((2, 0, 0), (3, 1, LANES - HALF)):
                parts = [
                    row_gather(lane_gather(cells[g][half], pick_y + start), rows_y)
                    for g in range(2)
                ]
                out_ref[base + side, dst, :] = jnp.where(quad < 2, parts[0], parts[1])
            for side, last in ((4, 0), (5, HALF - 1)):
                parts = [
                    row_gather(
                        jnp.where(
                            inner % 8 < 4,
                            lane_gather(cells[g][0], pick_z + last),
                            lane_gather(cells[g][1], pick_z + last),
                        ),
                        rows_z,
                    )
                    for g in range(2)
                ]
                out_ref[base + side, dst, :] = jnp.where(inner < 16, parts[0], parts[1])
        return 0

    lax.fori_loop(0, blocks, coarse_block, 0, unroll=2)


def primitives(cells):
    inverse = 1.0 / cells[0]
    kinetic = (
        0.5 * (cells[1] * cells[1] + cells[2] * cells[2] + cells[3] * cells[3]) * inverse
    )
    pressure = (adiabatic - 1.0) * (cells[4] - kinetic)
    sound = jnp.sqrt(adiabatic * pressure * inverse)
    return inverse, pressure, sound


def physical_flux(cells, normal, speed, pressure):
    entries = [
        cells[normal],
        cells[1] * speed,
        cells[2] * speed,
        cells[3] * speed,
        (cells[4] + pressure) * speed,
    ]
    entries[normal] = entries[normal] + pressure
    return entries


def face_flux(low, high, low_flux, high_flux, low_fast, high_fast):
    fastest = jnp.maximum(low_fast, high_fast)
    return [
        (low_flux[k] + high_flux[k]) - fastest * (high[k] - low[k]) for k in range(COMPS)
    ]


def add_steps(total, cells, normal, speed, pressure, fast, keep, step, axis):
    flux = physical_flux(cells, normal, speed, pressure)
    upper = face_flux(
        cells,
        [roll(c, -step, axis) for c in cells],
        flux,
        [roll(c, -step, axis) for c in flux],
        fast,
        roll(fast, -step, axis),
    )
    upper = [jnp.where(keep, c, 0.0) for c in upper]
    steps = [c - roll(c, step, axis) for c in upper]
    return steps if total is None else [total[k] + steps[k] for k in range(COMPS)]


def interior_kernel(
    boxes,
    fine_ref,
    partial_ref,
    restricted_ref,
    out_ref,
    coarse_ref,
    speed_ref,
    pressure_ref,
    fast_ref,
    pair_ref,
    sems,
):
    columns = FLAT // LANES
    row = iota((EDGE, LANES), 0)
    lane = iota((EDGE, LANES), 1)

    def column(step, _):
        box = step // columns
        at = pl.ds(pl.multiple_of((step % columns) * LANES, LANES), LANES)
        cells = [fine_ref[box, k, :, at] for k in range(COMPS)]
        inverse, pressure, sound = primitives(cells)
        speed_y = cells[2] * inverse
        there = pl.ds(pl.multiple_of(step * LANES, LANES), LANES)
        speed_ref[:, there] = speed_y
        pressure_ref[:, there] = pressure
        fast_ref[:, there] = jnp.abs(speed_y) + sound
        total = None
        for normal, axis, keep in ((1, 0, row < EDGE - 1), (3, 1, lane % EDGE < EDGE - 1)):
            speed = cells[normal] * inverse
            total = add_steps(
                total, cells, normal, speed, pressure, jnp.abs(speed) + sound, keep, 1, axis
            )
        for k in range(COMPS):
            out_ref[box, k, :, at] = total[k]
        return 0

    lax.fori_loop(0, boxes * columns, column, 0, unroll=2)
    wide = iota((8, FLAT), 1)

    def rows(step, _):
        box = step // 4
        at = pl.ds(pl.multiple_of((step % 4) * 8, 8), 8)
        along = pl.ds(pl.multiple_of(box * FLAT, FLAT), FLAT)
        cells = [fine_ref[box, k, at, :] for k in range(COMPS)]
        speed, pressure, fast = [ref[at, along] for ref in (speed_ref, pressure_ref, fast_ref)]
        total = [out_ref[box, k, at, :] for k in range(COMPS)]
        keep = wide < FLAT - EDGE
        total = add_steps(total, cells, 2, speed, pressure, fast, keep, EDGE, 1)
        for k in range(COMPS):
            out_ref[box, k, at, :] = cells[k] - (0.5 * courant) * total[k]
        return 0

    lax.fori_loop(0, boxes * 4, rows, 0)
    save = pltpu.make_async_copy(out_ref, partial_ref, sems.at[0])
    save.start()
    lane16 = iota((HALF, LANES), 1)
    pick = 64 * ((lane16 // HALF) % 2) + 2 * (lane16 % HALF)

    def restrict(step, _):
        box = step // COMPS
        comp = step % COMPS
        for h in range(2):
            total = jnp.zeros((HALF, LANES), jnp.float32)
            for w in range(4):
                v = 4 * h + w
                pair_ref[v] = out_ref[box, comp, :, LANES * v : LANES * v + LANES]
                pair = (
                    pair_ref[v, pl.ds(0, HALF, stride=2), :]
                    + pair_ref[v, pl.ds(1, HALF, stride=2), :]
                )
                pair = pair + roll(pair, -EDGE, 1)
                pair = pair + roll(pair, -1, 1)
                total = jnp.where(lane16 // 32 == w, lane_gather(pair, pick), total)
            coarse_ref[box, comp, :, LANES * h : LANES * h + LANES] = 0.125 * total
        return 0

    lax.fori_loop(0, boxes * COMPS, restrict, 0, unroll=2)
    last = pltpu.make_async_copy(coarse_ref, restricted_ref, sems.at[1])
    last.start()
    save.wait()
    last.wait()


def reply_kernel(code_ref, table_ref, out_ref, codes, sem, sems):
    slots = out_ref.shape[0]
    rows = table_ref.shape[0]
    copy = pltpu.make_async_copy(code_ref, codes, sem)
    copy.start()
    copy.wait()

    def each(act):
        for i in range(slots):
            code = codes[i, 0]

            @pl.when(code > 0)
            def _(i=i, code=code):
                source = table_ref.at[jnp.clip(code - 1, 0, rows - 1)]
                act(pltpu.make_async_copy(source, out_ref.at[i], sems.at[i]))

    each(lambda copy: copy.start())
    each(lambda copy: copy.wait())


def flux_kernel(
    boxes,
    blocks,
    line_size,
    fine_ids,
    coarse_ids,
    restricted_ref,
    table_ref,
    replies_ref,
    flux_ref,
    *rest,
):
    coarse_refs, (interior_ref, sem) = rest[:boxes], rest[boxes:]
    fetch = pltpu.make_async_copy(restricted_ref, interior_ref, sem)
    fetch.start()
    for face in range(6 * boxes):
        box, side = face // 6, face % 6
        normal = side // 2 + 1
        peer, _ = face_source(fine_ids, coarse_ids, box, side, boxes, blocks, line_size)
        own = [table_ref[face, 8 * k : 8 * k + 8, :] for k in range(COMPS)]
        ghost = [replies_ref[peer, 8 * k : 8 * k + 8, :] for k in range(COMPS)]
        sides = []
        for cells in (own, ghost):
            inverse, pressure, sound = primitives(cells)
            speed = cells[normal] * inverse
            flux = physical_flux(cells, normal, speed, pressure)
            sides.append((cells, flux, jnp.abs(speed) + sound))
        low, high = sides[::-1] if side % 2 == 0 else sides
        flux = face_flux(low[0], high[0], low[1], high[1], low[2], high[2])
        flux = [(0.5 * courant) * c for c in flux]
        for k in range(COMPS):
            flux_ref[face, 8 * k : 8 * k + 8, :] = flux[k]

    row = iota((8, LANES), 0)
    lane = iota((8, LANES), 1)
    even = 2 * (row % 4)

    def restrict(comp, box):
        at = slice(8 * comp, 8 * comp + 8)
        faces = [
            flux_ref[box * 6 + side, at, :] * (0.125 if side % 2 == 0 else -0.125)
            for side in range(6)
        ]
        for side in range(6):
            face = faces[side]
            if side < 2:
                face = face + roll(face, -1, 1)
                face = face + roll(face, -EDGE, 1)
                face = lane_gather(face, 64 * ((lane // HALF) % 2) + 2 * (lane % HALF))
            else:
                face = face + roll(face, -1, 0)
                face = face + roll(face, -1 if side < 4 else -EDGE, 1)
                face = row_gather(face, even)
            faces[side] = face
        for t in range(2):
            quarter = 2 * t + row // 4
            for h in range(2):
                spot = (comp, slice(8 * t, 8 * t + 8), slice(LANES * h, LANES * h + LANES))
                cells = interior_ref[(box,) + spot]
                pick = 64 * ((lane // HALF) % 2) + 8 * quarter + 4 * h + lane // 32
                cells = cells + jnp.where(lane % HALF == 0, lane_gather(faces[4], pick), 0.0)
                cells = cells + jnp.where(
                    lane % HALF == HALF - 1, lane_gather(faces[5], pick), 0.0
                )
                pick = 32 * quarter + 2 * (lane % HALF)
                near_edge = lane < HALF if h == 0 else lane >= LANES - HALF
                cells = cells + jnp.where(near_edge, lane_gather(faces[2 + h], pick), 0.0)
                first = row == 0 if t == 0 else row == 7
                cells = cells + jnp.where(first, row_gather(faces[t], 4 * h + lane // 32), 0.0)
                coarse_refs[box][spot] = cells

    fetch.wait()
    for box in range(boxes):
        for comp in range(COMPS):
            restrict(comp, box)


def finish_kernel(boxes, partial_ref, flux_ref, out_ref, next_ref, sems):
    row = iota((8, LANES), 0)
    lane = iota((8, LANES), 1)
    inner = lane % 32

    def plane(comp, _, box):
        at = pl.ds(pl.multiple_of(comp * 8, 8), 8)
        faces = [flux_ref[box * 6 + side, at, :] for side in range(6)]
        for q in range(4):
            for v in range(8):
                spot = (box, comp, slice(8 * q, 8 * q + 8), slice(LANES * v, LANES * v + LANES))
                cells = partial_ref[spot]
                shift = 8 * q + v
                cells = cells + jnp.where(inner == 0, roll(faces[4], -shift, 1), 0.0)
                cells = cells - jnp.where(inner == 31, roll(faces[5], 31 - shift, 1), 0.0)
                if v == 0:
                    cells = cells + jnp.where(lane < 32, roll(faces[2], -32 * q, 1), 0.0)
                if v == 7:
                    cells = cells - jnp.where(lane >= 96, roll(faces[3], 96 - 32 * q, 1), 0.0)
                if q == 0:
                    cells = cells + jnp.where(row == 0, faces[0][v : v + 1], 0.0)
                if q == 3:
                    cells = cells - jnp.where(row == 7, faces[1][v : v + 1], 0.0)
                next_ref[spot] = cells
        return 0

    copies = []
    for box in range(boxes):
        lax.fori_loop(0, COMPS, functools.partial(plane, box=box), 0)
        copy = pltpu.make_async_copy(next_ref.at[box], out_ref.at[box], sems.at[box])
        copy.start()
        copies.append(copy)
    for copy in copies:
        copy.wait()


def copy_kernel(x_ref, out_ref):
    out_ref[...] = x_ref[...]


def place_kernel(boxes, line_size, ring, covering_ref, _, *rest):
    sources = rest[: boxes * ring]
    out_ref, sems = rest[boxes * ring], rest[boxes * ring + 1]
    me = lax.axis_index("gx")
    blocks = out_ref.shape[0]

    for i in range(blocks):
        box = covering_ref[i]
        column = quotient(quotient(box, boxes), line_size)
        away = remainder(column - me + ring, ring)
        which = jnp.where(box >= 0, away * boxes + remainder(box, boxes), -1)
        for k in range(boxes * ring):

            @pl.when(which == k)
            def _(i=i, k=k):
                pltpu.make_async_copy(sources[k], out_ref.at[i], sems.at[i]).start()

    for i in range(blocks):

        @pl.when(covering_ref[i] >= 0)
        def _(i=i):
            pltpu.make_async_copy(sources[0], out_ref.at[i], sems.at[i]).wait()


def any_spec():
    return pl.BlockSpec(memory_space=pl.ANY)


def hbm_spec():
    return pl.BlockSpec(memory_space=pltpu.HBM)


def smem_spec():
    return pl.BlockSpec(memory_space=pltpu.SMEM)


def vmem_spec():
    return pl.BlockSpec(memory_space=pltpu.VMEM)


def kernel_params(mib=16):
    return pltpu.CompilerParams(vmem_limit_bytes=mib << 20)


def near(x):
    return pltpu.with_memory_space_constraint(x, pltpu.VMEM)


def far(x):
    return pltpu.with_memory_space_constraint(x, pltpu.HBM)


def exchange(x):
    return lax.all_to_all(x, PLANE, split_axis=0, concat_axis=0, tiled=True)


def body(fine_state, coarse_state, neighbours, coarse_sources, covering):
    boxes = fine_state.shape[0]
    blocks = coarse_state.shape[0]
    line_size = lax.axis_size("gy") * lax.axis_size("gz")
    ring = lax.axis_size("gx")
    f32 = jnp.float32

    requests = pl.pallas_call(
        functools.partial(request_kernel, boxes, blocks, line_size),
        out_shape=jax.ShapeDtypeStruct((line_size, LANES), jnp.int32),
        in_specs=[smem_spec(), smem_spec()],
        out_specs=vmem_spec(),
        name="requests",
    )(far(neighbours), far(coarse_sources))
    codes = exchange(requests)

    table = pl.pallas_call(
        functools.partial(table_kernel, boxes, blocks),
        out_shape=pltpu.VMEM((6 * (boxes + blocks), SLOT_ROWS, LANES), f32),
        in_specs=[vmem_spec(), vmem_spec()],
        out_specs=vmem_spec(),
        name="tables",
    )(fine_state, coarse_state)

    answers = pl.pallas_call(
        reply_kernel,
        out_shape=pltpu.HBM((line_size, SLOT_ROWS, LANES), f32),
        in_specs=[vmem_spec()] * 2,
        out_specs=hbm_spec(),
        scratch_shapes=[
            pltpu.SMEM((line_size, LANES), jnp.int32),
            pltpu.SemaphoreType.DMA,
            pltpu.SemaphoreType.DMA((line_size,)),
        ],
        compiler_params=kernel_params(),
        name="answers",
    )(near(codes), near(table))
    replies = exchange(answers)

    partial, interior = pl.pallas_call(
        functools.partial(interior_kernel, boxes),
        out_shape=(
            pltpu.HBM(fine_state.shape, f32),
            pltpu.HBM((boxes, COMPS, HALF, SMALL), f32),
        ),
        in_specs=[vmem_spec()],
        out_specs=(hbm_spec(), hbm_spec()),
        scratch_shapes=[
            pltpu.VMEM(fine_state.shape, f32),
            pltpu.VMEM((boxes, COMPS, HALF, SMALL), f32),
        ]
        + [pltpu.VMEM((EDGE, boxes * FLAT), f32)] * 3
        + [pltpu.VMEM((8, EDGE, LANES), f32), pltpu.SemaphoreType.DMA((2,))],
        compiler_params=kernel_params(),
        name="interior",
    )(fine_state)


    block = (COMPS, HALF, SMALL)
    flux, *restricted = pl.pallas_call(
        functools.partial(flux_kernel, boxes, blocks, line_size),
        out_shape=[pltpu.VMEM((6 * boxes, SLOT_ROWS, LANES), f32)]
        + [pltpu.VMEM(block, f32)] * boxes,
        in_specs=[smem_spec()] * 2 + [hbm_spec()] + [vmem_spec()] * 2,
        out_specs=[vmem_spec()] * (1 + boxes),
        scratch_shapes=[pltpu.VMEM((boxes,) + block, f32), pltpu.SemaphoreType.DMA],
        compiler_params=kernel_params(),
        name="fluxes",
    )(far(neighbours), far(coarse_sources), far(interior), near(table), near(replies))

    fine_next = pl.pallas_call(
        functools.partial(finish_kernel, boxes),
        out_shape=jax.ShapeDtypeStruct(fine_state.shape, f32),
        in_specs=[vmem_spec(), vmem_spec()],
        out_specs=any_spec(),
        scratch_shapes=[pltpu.VMEM(fine_state.shape, f32), pltpu.SemaphoreType.DMA((boxes,))],
        compiler_params=kernel_params(),
        name="finish",
    )(partial, near(flux))

    prior = pl.pallas_call(
        copy_kernel,
        out_shape=jax.ShapeDtypeStruct(coarse_state.shape, f32),
        in_specs=[vmem_spec()],
        out_specs=vmem_spec(),
        compiler_params=kernel_params(),
        name="prior",
    )(coarse_state)

    def shift(x, step):
        return lax.ppermute(x, "gx", [(i, (i + step) % ring) for i in range(ring)])

    gathered = {(0, b): restricted[b] for b in range(boxes)}
    right, left = list(restricted), list(restricted)
    half = ring // 2
    for hop in range(1, half + 1):
        for b in range(boxes):
            if 2 * hop < ring or b % 2 == 0:
                right[b] = shift(right[b], 1)
                gathered[ring - hop, b] = right[b]
            if 2 * hop < ring or b % 2 == 1:
                left[b] = shift(left[b], -1)
                gathered[hop, b] = left[b]

    coarse_next = pl.pallas_call(
        functools.partial(place_kernel, boxes, line_size, ring),
        out_shape=jax.ShapeDtypeStruct(coarse_state.shape, f32),
        in_specs=[smem_spec(), any_spec()] + [vmem_spec()] * (boxes * ring),
        out_specs=any_spec(),
        scratch_shapes=[pltpu.SemaphoreType.DMA((blocks,))],
        input_output_aliases={1: 0},
        compiler_params=kernel_params(),
        name="place",
    )(
        far(covering),
        prior,
        *[near(gathered[k, b]) for k in range(ring) for b in range(boxes)],
    )
    return fine_next, coarse_next


def solution(mesh):
    spec = P(AXES)
    return jax.shard_map(
        body, mesh=mesh, in_specs=(spec,) * 5, out_specs=(spec, spec), check_vma=False
    )
```

```python
import functools

import jax
import jax.numpy as jnp
from jax import lax
from jax.experimental import pallas as pl
from jax.experimental.pallas import tpu as pltpu
from jax.sharding import PartitionSpec as P


adiabatic = 5.0 / 3.0
courant = 0.12
AXES = ("gx", "gy", "gz")
PLANE = ("gy", "gz")

EDGE = 32
HALF = 16
FLAT = EDGE * EDGE
SMALL = HALF * HALF
LANES = 128
COMPS = 5
SLOT_ROWS = COMPS * FLAT // LANES


def iota(shape, dim):
    return lax.broadcasted_iota(jnp.int32, shape, dim)


def roll(x, shift, axis):
    size = x.shape[axis]
    shift = shift % size
    return x if shift == 0 else pltpu.roll(x, shift, axis)


def quotient(x, n):
    return lax.shift_right_logical(x, n.bit_length() - 1) if n & (n - 1) == 0 else lax.div(x, n)


def remainder(x, n):
    return lax.bitwise_and(x, n - 1) if n & (n - 1) == 0 else lax.rem(x, n)


def face_source(fine_ref, coarse_ref, box, side, boxes, blocks, line_size):
    fine_id = fine_ref[box, side]
    coarse_id = coarse_ref[box, side]
    is_fine = fine_id >= 0
    device = jnp.where(is_fine, quotient(fine_id, boxes), quotient(coarse_id, blocks))
    row = jnp.where(
        is_fine,
        remainder(fine_id, boxes) * 6 + (side ^ 1),
        boxes * 6 + remainder(coarse_id, blocks) * 6 + (side ^ 1),
    )
    return remainder(device, line_size), row


def request_kernel(boxes, blocks, line_size, fine_ref, coarse_ref, out_ref):
    peers = iota(out_ref.shape, 0)
    table = jnp.zeros(out_ref.shape, jnp.int32)
    for box in range(boxes):
        for side in range(6):
            peer, row = face_source(fine_ref, coarse_ref, box, side, boxes, blocks, line_size)
            table = jnp.where(peers == peer, row + 1, table)
    out_ref[...] = table


def lane_gather(x, index):
    return jnp.take_along_axis(x, index, axis=1)


def row_gather(x, index):
    return jnp.take_along_axis(x, index, axis=0)


def table_kernel(boxes, blocks, fine_hbm, coarse_hbm, out_ref, fine_ref, coarse_ref, sems):
    loads = [
        pltpu.make_async_copy(fine_hbm.at[box], fine_ref.at[box], sems.at[box])
        for box in range(boxes)
    ]
    loads.append(pltpu.make_async_copy(coarse_hbm, coarse_ref, sems.at[boxes]))
    for load in loads:
        load.start()
    row = iota((8, LANES), 0)
    lane = iota((8, LANES), 1)
    quad = lane // 32
    inner = lane % 32

    def fine_box(box):
        base = box * 6
        for comp in range(COMPS):
            dst = slice(8 * comp, 8 * comp + 8)
            for side, first in ((0, 0), (1, EDGE - 1)):
                for r in range(8):
                    out_ref[base + side, 8 * comp + r : 8 * comp + r + 1, :] = fine_ref[
                        box, comp, first : first + 1, LANES * r : LANES * r + LANES
                    ]
            y_low = jnp.zeros((8, LANES), jnp.float32)
            y_high = y_low
            z_low = y_low
            z_high = y_low
            for q in range(4):
                for v in range(8):
                    cells = fine_ref[box, comp, 8 * q : 8 * q + 8, LANES * v : LANES * v + LANES]
                    if v == 0:
                        y_low = jnp.where(quad == q, roll(cells, 32 * q, 1), y_low)
                    if v == 7:
                        y_high = jnp.where(quad == q, roll(cells, 32 * q - 96, 1), y_high)
                    spot = inner == 8 * q + v
                    z_low = jnp.where(spot, roll(cells, 8 * q + v, 1), z_low)
                    z_high = jnp.where(spot, roll(cells, 8 * q + v - 31, 1), z_high)
            out_ref[base + 2, dst, :] = y_low
            out_ref[base + 3, dst, :] = y_high
            out_ref[base + 4, dst, :] = z_low
            out_ref[base + 5, dst, :] = z_high

    for box in range(boxes):
        loads[box].wait()
        fine_box(box)
    loads[boxes].wait()

    pick_x = 32 * (row % 4) + 16 * (quad // 2) + inner // 2
    pick_y = inner // 2
    pick_z = 32 * (inner % 4) + 16 * (quad // 2)
    rows_y = 4 * (quad % 2) + row // 2
    rows_z = 4 * ((inner // 8) % 2) + row // 2

    def coarse_block(block, _):
        base = boxes * 6 + block * 6
        for comp in range(COMPS):
            dst = slice(8 * comp, 8 * comp + 8)
            cells = [
                [
                    coarse_ref[block, comp, 8 * g : 8 * g + 8, LANES * h : LANES * h + LANES]
                    for h in range(2)
                ]
                for g in range(2)
            ]
            for side, first in ((0, 0), (1, HALF - 1)):
                parts = [
                    jnp.broadcast_to(cells[first // 8][h][first % 8 : first % 8 + 1], (8, LANES))
                    for h in range(2)
                ]
                out_ref[base + side, dst, :] = jnp.where(
                    row < 4, lane_gather(parts[0], pick_x), lane_gather(parts[1], pick_x)
                )
            for side, half, start in ((2, 0, 0), (3, 1, LANES - HALF)):
                parts = [
                    row_gather(lane_gather(cells[g][half], pick_y + start), rows_y)
                    for g in range(2)
                ]
                out_ref[base + side, dst, :] = jnp.where(quad < 2, parts[0], parts[1])
            for side, last in ((4, 0), (5, HALF - 1)):
                parts = [
                    row_gather(
                        jnp.where(
                            inner % 8 < 4,
                            lane_gather(cells[g][0], pick_z + last),
                            lane_gather(cells[g][1], pick_z + last),
                        ),
                        rows_z,
                    )
                    for g in range(2)
                ]
                out_ref[base + side, dst, :] = jnp.where(inner < 16, parts[0], parts[1])
        return 0

    lax.fori_loop(0, blocks, coarse_block, 0, unroll=2)


def primitives(cells):
    inverse = 1.0 / cells[0]
    kinetic = (
        0.5 * (cells[1] * cells[1] + cells[2] * cells[2] + cells[3] * cells[3]) * inverse
    )
    pressure = (adiabatic - 1.0) * (cells[4] - kinetic)
    sound = jnp.sqrt(adiabatic * pressure * inverse)
    return inverse, pressure, sound


def physical_flux(cells, normal, speed, pressure):
    entries = [
        cells[normal],
        cells[1] * speed,
        cells[2] * speed,
        cells[3] * speed,
        (cells[4] + pressure) * speed,
    ]
    entries[normal] = entries[normal] + pressure
    return entries


def face_flux(low, high, low_flux, high_flux, low_fast, high_fast):
    fastest = jnp.maximum(low_fast, high_fast)
    return [
        (low_flux[k] + high_flux[k]) - fastest * (high[k] - low[k]) for k in range(COMPS)
    ]


def add_steps(total, cells, normal, speed, pressure, fast, keep, step, axis):
    flux = physical_flux(cells, normal, speed, pressure)
    upper = face_flux(
        cells,
        [roll(c, -step, axis) for c in cells],
        flux,
        [roll(c, -step, axis) for c in flux],
        fast,
        roll(fast, -step, axis),
    )
    upper = [jnp.where(keep, c, 0.0) for c in upper]
    steps = [c - roll(c, step, axis) for c in upper]
    return steps if total is None else [total[k] + steps[k] for k in range(COMPS)]


def interior_kernel(
    boxes,
    fine_ref,
    partial_ref,
    coarse_ref,
    out_ref,
    speed_ref,
    pressure_ref,
    fast_ref,
    pair_ref,
    sem,
):
    columns = FLAT // LANES
    row = iota((EDGE, LANES), 0)
    lane = iota((EDGE, LANES), 1)

    def column(step, _):
        box = step // columns
        at = pl.ds(pl.multiple_of((step % columns) * LANES, LANES), LANES)
        cells = [fine_ref[box, k, :, at] for k in range(COMPS)]
        inverse, pressure, sound = primitives(cells)
        speed_y = cells[2] * inverse
        there = pl.ds(pl.multiple_of(step * LANES, LANES), LANES)
        speed_ref[:, there] = speed_y
        pressure_ref[:, there] = pressure
        fast_ref[:, there] = jnp.abs(speed_y) + sound
        total = None
        for normal, axis, keep in ((1, 0, row < EDGE - 1), (3, 1, lane % EDGE < EDGE - 1)):
            speed = cells[normal] * inverse
            total = add_steps(
                total, cells, normal, speed, pressure, jnp.abs(speed) + sound, keep, 1, axis
            )
        for k in range(COMPS):
            out_ref[box, k, :, at] = total[k]
        return 0

    lax.fori_loop(0, boxes * columns, column, 0, unroll=2)
    wide = iota((8, FLAT), 1)

    def rows(step, _):
        box = step // 4
        at = pl.ds(pl.multiple_of((step % 4) * 8, 8), 8)
        along = pl.ds(pl.multiple_of(box * FLAT, FLAT), FLAT)
        cells = [fine_ref[box, k, at, :] for k in range(COMPS)]
        speed, pressure, fast = [ref[at, along] for ref in (speed_ref, pressure_ref, fast_ref)]
        total = [out_ref[box, k, at, :] for k in range(COMPS)]
        keep = wide < FLAT - EDGE
        total = add_steps(total, cells, 2, speed, pressure, fast, keep, EDGE, 1)
        for k in range(COMPS):
            out_ref[box, k, at, :] = cells[k] - (0.5 * courant) * total[k]
        return 0

    lax.fori_loop(0, boxes * 4, rows, 0)
    save = pltpu.make_async_copy(out_ref, partial_ref, sem)
    save.start()
    lane16 = iota((HALF, LANES), 1)
    pick = 64 * ((lane16 // HALF) % 2) + 2 * (lane16 % HALF)

    def restrict(step, _):
        box = step // COMPS
        comp = step % COMPS
        for h in range(2):
            total = jnp.zeros((HALF, LANES), jnp.float32)
            for w in range(4):
                v = 4 * h + w
                pair_ref[v] = out_ref[box, comp, :, LANES * v : LANES * v + LANES]
                pair = (
                    pair_ref[v, pl.ds(0, HALF, stride=2), :]
                    + pair_ref[v, pl.ds(1, HALF, stride=2), :]
                )
                pair = pair + roll(pair, -EDGE, 1)
                pair = pair + roll(pair, -1, 1)
                total = jnp.where(lane16 // 32 == w, lane_gather(pair, pick), total)
            coarse_ref[box, comp, :, LANES * h : LANES * h + LANES] = 0.125 * total
        return 0

    lax.fori_loop(0, boxes * COMPS, restrict, 0, unroll=2)
    save.wait()


def reply_kernel(code_ref, table_ref, out_ref, codes, sem, sems):
    slots = out_ref.shape[0]
    rows = table_ref.shape[0]
    copy = pltpu.make_async_copy(code_ref, codes, sem)
    copy.start()
    copy.wait()

    def each(act):
        for i in range(slots):
            code = codes[i, 0]

            @pl.when(code > 0)
            def _(i=i, code=code):
                source = table_ref.at[jnp.clip(code - 1, 0, rows - 1)]
                act(pltpu.make_async_copy(source, out_ref.at[i], sems.at[i]))

    each(lambda copy: copy.start())
    each(lambda copy: copy.wait())


def flux_kernel(
    boxes,
    blocks,
    line_size,
    fine_hbm,
    coarse_hbm,
    interior_ref,
    table_ref,
    replies_ref,
    flux_ref,
    *rest,
):
    coarse_refs, (fine_ids, coarse_ids, sems) = rest[:boxes], rest[boxes:]
    loads = [
        pltpu.make_async_copy(fine_hbm, fine_ids, sems.at[0]),
        pltpu.make_async_copy(coarse_hbm, coarse_ids, sems.at[1]),
    ]
    for load in loads:
        load.start()

    def half_state(cells, normal):
        inverse, pressure, sound = primitives(cells)
        speed = cells[normal] * inverse
        return cells, physical_flux(cells, normal, speed, pressure), jnp.abs(speed) + sound

    own = []
    for face in range(6 * boxes):
        cells = [table_ref[face, 8 * k : 8 * k + 8, :] for k in range(COMPS)]
        own.append(half_state(cells, face % 6 // 2 + 1))
    for load in loads:
        load.wait()
    for face in range(6 * boxes):
        box, side = face // 6, face % 6
        peer, _ = face_source(fine_ids, coarse_ids, box, side, boxes, blocks, line_size)
        cells = [replies_ref[peer, 8 * k : 8 * k + 8, :] for k in range(COMPS)]
        ghost = half_state(cells, side // 2 + 1)
        low, high = (ghost, own[face]) if side % 2 == 0 else (own[face], ghost)
        flux = face_flux(low[0], high[0], low[1], high[1], low[2], high[2])
        for k in range(COMPS):
            flux_ref[face, 8 * k : 8 * k + 8, :] = (0.5 * courant) * flux[k]

    row = iota((8, LANES), 0)
    lane = iota((8, LANES), 1)
    even = 2 * (row % 4)

    def restrict(comp, box):
        at = slice(8 * comp, 8 * comp + 8)
        faces = [
            flux_ref[box * 6 + side, at, :] * (0.125 if side % 2 == 0 else -0.125)
            for side in range(6)
        ]
        for side in range(6):
            face = faces[side]
            if side < 2:
                face = face + roll(face, -1, 1)
                face = face + roll(face, -EDGE, 1)
                face = lane_gather(face, 64 * ((lane // HALF) % 2) + 2 * (lane % HALF))
            else:
                face = face + roll(face, -1, 0)
                face = face + roll(face, -1 if side < 4 else -EDGE, 1)
                face = row_gather(face, even)
            faces[side] = face
        for t in range(2):
            quarter = 2 * t + row // 4
            for h in range(2):
                spot = (comp, slice(8 * t, 8 * t + 8), slice(LANES * h, LANES * h + LANES))
                cells = interior_ref[(box,) + spot]
                pick = 64 * ((lane // HALF) % 2) + 8 * quarter + 4 * h + lane // 32
                cells = cells + jnp.where(lane % HALF == 0, lane_gather(faces[4], pick), 0.0)
                cells = cells + jnp.where(
                    lane % HALF == HALF - 1, lane_gather(faces[5], pick), 0.0
                )
                pick = 32 * quarter + 2 * (lane % HALF)
                near_edge = lane < HALF if h == 0 else lane >= LANES - HALF
                cells = cells + jnp.where(near_edge, lane_gather(faces[2 + h], pick), 0.0)
                first = row == 0 if t == 0 else row == 7
                cells = cells + jnp.where(first, row_gather(faces[t], 4 * h + lane // 32), 0.0)
                coarse_refs[box][spot] = cells

    for box in range(boxes):
        for comp in range(COMPS):
            restrict(comp, box)


def finish_kernel(boxes, partial_ref, flux_ref, out_ref, next_ref, sems):
    row = iota((8, LANES), 0)
    lane = iota((8, LANES), 1)
    inner = lane % 32

    def plane(comp, _, box):
        at = pl.ds(pl.multiple_of(comp * 8, 8), 8)
        faces = [flux_ref[box * 6 + side, at, :] for side in range(6)]
        for q in range(4):
            for v in range(8):
                spot = (box, comp, slice(8 * q, 8 * q + 8), slice(LANES * v, LANES * v + LANES))
                cells = partial_ref[spot]
                shift = 8 * q + v
                cells = cells + jnp.where(inner == 0, roll(faces[4], -shift, 1), 0.0)
                cells = cells - jnp.where(inner == 31, roll(faces[5], 31 - shift, 1), 0.0)
                if v == 0:
                    cells = cells + jnp.where(lane < 32, roll(faces[2], -32 * q, 1), 0.0)
                if v == 7:
                    cells = cells - jnp.where(lane >= 96, roll(faces[3], 96 - 32 * q, 1), 0.0)
                if q == 0:
                    cells = cells + jnp.where(row == 0, faces[0][v : v + 1], 0.0)
                if q == 3:
                    cells = cells - jnp.where(row == 7, faces[1][v : v + 1], 0.0)
                next_ref[spot] = cells
        return 0

    copies = []
    for box in range(boxes):
        lax.fori_loop(0, COMPS, functools.partial(plane, box=box), 0)
        copy = pltpu.make_async_copy(next_ref.at[box], out_ref.at[box], sems.at[box])
        copy.start()
        copies.append(copy)
    for copy in copies:
        copy.wait()


def copy_kernel(x_ref, out_ref):
    out_ref[...] = x_ref[...]


def place_kernel(boxes, line_size, ring, covering_ref, _, *rest):
    sources = rest[: boxes * ring]
    out_ref, sems = rest[boxes * ring], rest[boxes * ring + 1]
    me = lax.axis_index("gx")
    blocks = out_ref.shape[0]

    for i in range(blocks):
        box = covering_ref[i]

        @pl.when(box >= 0)
        def _(i=i, box=box):
            column = quotient(quotient(box, boxes), line_size)
            away = remainder(column - me + ring, ring)
            which = away * boxes + remainder(box, boxes)
            for k in range(boxes * ring):

                @pl.when(which == k)
                def _(k=k):
                    pltpu.make_async_copy(sources[k], out_ref.at[i], sems.at[i]).start()

    for i in range(blocks):

        @pl.when(covering_ref[i] >= 0)
        def _(i=i):
            pltpu.make_async_copy(sources[0], out_ref.at[i], sems.at[i]).wait()


def any_spec():
    return pl.BlockSpec(memory_space=pl.ANY)


def hbm_spec():
    return pl.BlockSpec(memory_space=pltpu.HBM)


def smem_spec():
    return pl.BlockSpec(memory_space=pltpu.SMEM)


def vmem_spec():
    return pl.BlockSpec(memory_space=pltpu.VMEM)


def kernel_params(mib=16):
    return pltpu.CompilerParams(vmem_limit_bytes=mib << 20)


def near(x):
    return pltpu.with_memory_space_constraint(x, pltpu.VMEM)


def far(x):
    return pltpu.with_memory_space_constraint(x, pltpu.HBM)


def exchange(x):
    return lax.all_to_all(x, PLANE, split_axis=0, concat_axis=0, tiled=True)


def body(fine_state, coarse_state, neighbours, coarse_sources, covering):
    boxes = fine_state.shape[0]
    blocks = coarse_state.shape[0]
    line_size = lax.axis_size("gy") * lax.axis_size("gz")
    ring = lax.axis_size("gx")
    f32 = jnp.float32

    requests = pl.pallas_call(
        functools.partial(request_kernel, boxes, blocks, line_size),
        out_shape=jax.ShapeDtypeStruct((line_size, LANES), jnp.int32),
        in_specs=[smem_spec(), smem_spec()],
        out_specs=vmem_spec(),
        name="requests",
    )(far(neighbours), far(coarse_sources))
    codes = exchange(requests)

    table = pl.pallas_call(
        functools.partial(table_kernel, boxes, blocks),
        out_shape=pltpu.VMEM((6 * (boxes + blocks), SLOT_ROWS, LANES), f32),
        in_specs=[hbm_spec(), hbm_spec()],
        out_specs=vmem_spec(),
        scratch_shapes=[
            pltpu.VMEM(fine_state.shape, f32),
            pltpu.VMEM(coarse_state.shape, f32),
            pltpu.SemaphoreType.DMA((boxes + 1,)),
        ],
        name="tables",
    )(far(fine_state), far(coarse_state))

    answers = pl.pallas_call(
        reply_kernel,
        out_shape=pltpu.HBM((line_size, SLOT_ROWS, LANES), f32),
        in_specs=[vmem_spec()] * 2,
        out_specs=hbm_spec(),
        scratch_shapes=[
            pltpu.SMEM((line_size, LANES), jnp.int32),
            pltpu.SemaphoreType.DMA,
            pltpu.SemaphoreType.DMA((line_size,)),
        ],
        compiler_params=kernel_params(),
        name="answers",
    )(near(codes), near(table))
    replies = exchange(answers)

    partial, interior = pl.pallas_call(
        functools.partial(interior_kernel, boxes),
        out_shape=(
            pltpu.HBM(fine_state.shape, f32),
            pltpu.VMEM((boxes, COMPS, HALF, SMALL), f32),
        ),
        in_specs=[vmem_spec()],
        out_specs=(hbm_spec(), vmem_spec()),
        scratch_shapes=[
            pltpu.VMEM(fine_state.shape, f32),
        ]
        + [pltpu.VMEM((EDGE, boxes * FLAT), f32)] * 3
        + [pltpu.VMEM((8, EDGE, LANES), f32), pltpu.SemaphoreType.DMA],
        compiler_params=kernel_params(),
        name="interior",
    )(fine_state)


    block = (COMPS, HALF, SMALL)
    flux, *restricted = pl.pallas_call(
        functools.partial(flux_kernel, boxes, blocks, line_size),
        out_shape=[pltpu.VMEM((6 * boxes, SLOT_ROWS, LANES), f32)]
        + [pltpu.VMEM(block, f32)] * boxes,
        in_specs=[hbm_spec()] * 2 + [vmem_spec()] * 3,
        out_specs=[vmem_spec()] * (1 + boxes),
        scratch_shapes=[pltpu.SMEM(neighbours.shape, jnp.int32)] * 2
        + [pltpu.SemaphoreType.DMA((2,))],
        compiler_params=kernel_params(),
        name="fluxes",
    )(far(neighbours), far(coarse_sources), near(interior), near(table), near(replies))

    fine_next = pl.pallas_call(
        functools.partial(finish_kernel, boxes),
        out_shape=jax.ShapeDtypeStruct(fine_state.shape, f32),
        in_specs=[vmem_spec(), vmem_spec()],
        out_specs=any_spec(),
        scratch_shapes=[pltpu.VMEM(fine_state.shape, f32), pltpu.SemaphoreType.DMA((boxes,))],
        compiler_params=kernel_params(),
        name="finish",
    )(partial, near(flux))

    prior = pl.pallas_call(
        copy_kernel,
        out_shape=jax.ShapeDtypeStruct(coarse_state.shape, f32),
        in_specs=[vmem_spec()],
        out_specs=vmem_spec(),
        compiler_params=kernel_params(),
        name="prior",
    )(coarse_state)

    def shift(x, step):
        return lax.ppermute(x, "gx", [(i, (i + step) % ring) for i in range(ring)])

    gathered = {(0, b): restricted[b] for b in range(boxes)}
    right, left = list(restricted), list(restricted)
    half = ring // 2
    for hop in range(1, half + 1):
        for b in range(boxes):
            if 2 * hop < ring or b % 2 == 0:
                right[b] = shift(right[b], 1)
                gathered[ring - hop, b] = right[b]
            if 2 * hop < ring or b % 2 == 1:
                left[b] = shift(left[b], -1)
                gathered[hop, b] = left[b]

    coarse_next = pl.pallas_call(
        functools.partial(place_kernel, boxes, line_size, ring),
        out_shape=jax.ShapeDtypeStruct(coarse_state.shape, f32),
        in_specs=[smem_spec(), any_spec()] + [vmem_spec()] * (boxes * ring),
        out_specs=any_spec(),
        scratch_shapes=[pltpu.SemaphoreType.DMA((blocks,))],
        input_output_aliases={1: 0},
        compiler_params=kernel_params(),
        name="place",
    )(
        pltpu.with_memory_space_constraint(covering, pltpu.SMEM),
        prior,
        *[near(gathered[k, b]) for k in range(ring) for b in range(boxes)],
    )
    return fine_next, coarse_next


def solution(mesh):
    spec = P(AXES)
    return jax.shard_map(
        body, mesh=mesh, in_specs=(spec,) * 5, out_specs=(spec, spec), check_vma=False
    )
```
